32 devices in a mesh: groups: 2 (over y), rows: 4 (over z), cols: 2 (over x), sub: 2 (over core).
Axes of the slice: x: 2, y: 2, z: 4, core: 2. Of those that a mesh axis runs over, the one named last changes fastest.
Arguments:
- elevation: float32 [256, 16384], P(('groups', 'rows', 'sub'), 'cols'), parts along dimension 0, may hold values from -6 to 6
- fill_depth: float32 [256, 16384], P(('groups', 'rows', 'sub'), 'cols'), parts along dimension 0, may hold values from 0.5 to 4
- edge_rows: int32 [4, 16384], P('groups', 'cols'), parts along dimension 0, may hold values 0 or 1
- edge_sides: int32 [4, 128], P('groups', ('rows', 'sub')), parts along dimension 0, may hold values 0 or 1
- adjacency: int32 [16, 6], P('groups'), parts along dimension 0, may hold values from 0 to 7
Outputs:
- filled: float32 [256, 16384], P(('groups', 'rows', 'sub'), 'cols'), parts along dimension 0
The draws below stay inside these ranges and needn't reach their ends.
There are 2 independent parts, one for each index of `groups`. The reference program is written for one: setup_inputs(seed, part) draws one part's arguments, and reference() takes and returns one part's arrays. A program takes and returns all parts, laid end to end along the dimension named above; each array names one. Nothing has to cross between parts.
Inputs may be any that keep to these rules, and one draw needn't show every extreme that they name: `adjacency`: tile numbers count tiles row by row.
All inputs are finite; a program needn't handle non-finite values. No bound on the sum of `edge_rows` or of `edge_sides` on one device may be relied on, other than what follows from the above.
Results may differ from the reference program's by a relative error of at most 0.00002.
Values sent between devices are 32-bit elements; how exact they have to be, the bound alone decides.
A program may use at most 64 MiB of HBM per device.

```python
import math
import jax
import jax.numpy as jnp

PASSES = 8
FINAL = 4
ROUNDS = 4
DEG = 6
NR = 128
NC = 16384
TILES = 8
N_ROWS = 4
N_COLS = 2


def with_ends(drawn, own_key, smallest, largest):
    shape = drawn.shape
    place = [jax.random.randint(jax.random.fold_in(own_key, axis), (), 0, shape[axis]) for axis in range(len(shape))]
    drawn = drawn.at[tuple(place)].set(smallest)
    longest = shape.index(max(shape))
    place[longest] = (place[longest] + 1) % shape[longest]
    return drawn.at[tuple(place)].set(largest)


def steps_of(stream_key, shape, pieces, least, largest):
    def one(dim, blocks):
        draws = jax.random.uniform(jax.random.fold_in(jax.random.fold_in(stream_key, 6), dim), (blocks,), jnp.float32, least / len(pieces), largest / len(pieces))
        return jnp.repeat(jnp.exp(draws), shape[dim] // blocks).reshape((-1,) + (1,) * (len(shape) - dim - 1))

    factor_of = one(*pieces[0])
    for cut in pieces[1:]:
        factor_of = factor_of * one(*cut)
    return factor_of


def noise(key, shape, scale, limit, split=(), dtype=jnp.bfloat16):
    array = jax.random.normal(key, shape, jnp.float32) * scale
    if len(split) > 0:
        array = steps_of(key, shape, split, -0.22, 0.18) * array
    return jnp.clip(array, min=-limit, max=limit).astype(dtype)


def setup_inputs(seed: int = 0, part: int = 0) -> dict:
    seeds = jax.random.split(jax.random.key(seed), 6)
    part_keys = jax.random.split(jax.random.fold_in(seeds[5], part), 6)
    elevation = noise(part_keys[0], (NR, NC), 1.0, 6.0, ((0, 8), (1, 2)), jnp.float32)
    fill_depth = jnp.clip(jnp.exp(math.log(4.0) - 2.0794415 * jax.random.uniform(part_keys[1], (NR, NC), jnp.float32) ** steps_of(part_keys[1], (NR, NC), ((0, 8), (1, 2)), -0.2, 0.2)), 0.5, 4.0)
    edge_rows = with_ends((jax.random.randint(part_keys[2], (2, NC), 0, 8) < 1).astype(jnp.int32), jax.random.fold_in(part_keys[2], 1), 0, 1)
    edge_sides = with_ends((jax.random.randint(part_keys[3], (2, NR), 0, 8) < 1).astype(jnp.int32), jax.random.fold_in(part_keys[3], 1), 0, 1)
    adjacency = with_ends(jax.random.randint(part_keys[4], (TILES, DEG), 0, TILES), jax.random.fold_in(part_keys[4], 1), 0, TILES - 1).astype(jnp.int32)
    return dict(elevation=elevation, fill_depth=fill_depth, edge_rows=edge_rows, edge_sides=edge_sides, adjacency=adjacency)


unreached = 1.0e9
rise_step = 0.01
hop_rise = 0.05
spill_lift = 3.0


def neighbour_min(padded):
    height = padded.shape[0] - 2
    width = padded.shape[1] - 2
    lowest = None
    for shift_row in range(3):
        for shift_col in range(3):
            if shift_row == 1 and shift_col == 1:
                continue
            piece = padded[shift_row:shift_row + height, shift_col:shift_col + width]
            lowest = piece if lowest is None else jnp.minimum(lowest, piece)
    return lowest


def relax(surface, ground):
    padded = jnp.pad(surface, 1, constant_values=unreached)
    lowest = neighbour_min(padded)
    return jnp.maximum(ground, jnp.minimum(surface, lowest + rise_step))


def reference(elevation, fill_depth, edge_rows, edge_sides, adjacency):
    total_rows, total_cols = elevation.shape
    row_ids = jnp.arange(total_rows)[:, None]
    col_ids = jnp.arange(total_cols)[None, :]
    outlet = ((row_ids == 0) & (edge_rows[0][None, :] == 1)) | ((row_ids == total_rows - 1) & (edge_rows[1][None, :] == 1))
    outlet = outlet | ((col_ids == 0) & (edge_sides[0][:, None] == 1)) | ((col_ids == total_cols - 1) & (edge_sides[1][:, None] == 1))
    surface = jnp.where(outlet, elevation, elevation + fill_depth)
    for step in range(PASSES):
        surface = relax(surface, elevation)
    tile_rows = total_rows // N_ROWS
    tile_cols = total_cols // N_COLS
    blocks = surface.reshape(N_ROWS, tile_rows, N_COLS, tile_cols)
    floors = jnp.minimum(jnp.min(blocks[:, 0, :, :], axis=-1), jnp.min(blocks[:, -1, :, :], axis=-1))
    floors = jnp.minimum(floors, jnp.min(blocks[:, :, :, 0], axis=1))
    floors = jnp.minimum(floors, jnp.min(blocks[:, :, :, -1], axis=1))
    level = floors.reshape(N_ROWS * N_COLS)
    for step in range(ROUNDS):
        level = jnp.minimum(level, jnp.min(level[adjacency], axis=1) + hop_rise)
    ceiling = (level + spill_lift).reshape(N_ROWS, 1, N_COLS, 1)
    blocks = jnp.maximum(elevation.reshape(N_ROWS, tile_rows, N_COLS, tile_cols), jnp.minimum(blocks, ceiling))
    surface = blocks.reshape(total_rows, total_cols)
    for step in range(FINAL):
        surface = relax(surface, elevation)
    return surface
```

```python
import functools

import jax
import jax.numpy as jnp
from jax import lax
from jax.experimental import pallas as pl
from jax.experimental.pallas import tpu as pltpu
from jax.sharding import PartitionSpec as P

PASSES = 8
ROUNDS = 4

unreached = 1000000000.0
rise_step = 0.01
hop_rise = 0.05
spill_lift = 3.0

DEPTH = 4
SUBL = 8
TILE = 128
HALF = TILE // 2
MESH = pl.DeviceIdType.MESH


def kernel(
    sizes, elev_hbm, fill_hbm, edge_hbm, side_hbm, adj_hbm, out_hbm,
    ground, fill, first, second, third, ping, pong, done,
    edge, side, adj, ring_own, ring_low, ring_high,
    mine, gathered, hops, levels, even, odd, seam_ground,
    load_sem, send_sem, recv_sem, level_send, level_recv, out_sem,
):
    n_groups, n_rows, n_cols, n_sub = sizes
    height, width = elev_hbm.shape
    chunk = width // SUBL
    lanes = chunk + TILE
    low, high = DEPTH, DEPTH + height
    total = height + 2 * DEPTH
    n_tiles = adj.shape[0]
    padded = mine.shape[1]
    members = n_rows * n_cols * n_sub

    group = lax.axis_index("groups")
    tile_row = lax.axis_index("rows")
    col = lax.axis_index("cols")
    sub = lax.axis_index("sub")
    band = tile_row * n_sub + sub
    bands = n_rows * n_sub
    me = (tile_row * n_cols + col) * n_sub + sub

    near = 1 - 2 * (band % 2)
    far = -near

    def has(dr):
        return jnp.logical_and(band + dr >= 0, band + dr < bands)

    has_col = {-1: col > 0, 1: col < n_cols - 1}

    def both(dr, dc):
        if dc == 0:
            return has(dr)
        if isinstance(dr, int) and dr == 0:
            return has_col[dc]
        return jnp.logical_and(has(dr), has_col[dc])

    def device(dr, dc):
        to_band = band + dr
        return (group, to_band // n_sub, col + dc, to_band % n_sub)

    barrier = pltpu.get_barrier_semaphore()

    def member(number):
        return (group, number // (n_sub * n_cols), (number // n_sub) % n_cols, number % n_sub)

    def greet(step, carry):
        pl.semaphore_signal(
            barrier, inc=1, device_id=member((me + step) % members), device_id_type=MESH
        )
        return carry

    lax.fori_loop(1, members, greet, 0)

    loads = []
    for number, (src, dst, at) in enumerate(
        ((elev_hbm, ground, low), (fill_hbm, fill, 0), (edge_hbm, edge, 0))
    ):
        count = src.shape[0]
        for s in range(SUBL):
            pltpu.make_async_copy(
                src.at[:, pl.ds(s * chunk, chunk)],
                dst.at[pl.ds(at, count), s, pl.ds(0, chunk)],
                load_sem.at[number],
            ).start()
        whole = dst.at[pl.ds(at, count), :, pl.ds(0, chunk)]
        loads.append(pltpu.make_async_copy(whole, whole, load_sem.at[number]))
    side_load = pltpu.make_async_copy(side_hbm, side, load_sem.at[3])
    side_load.start()
    adj_load = pltpu.make_async_copy(adj_hbm, adj, load_sem.at[4])
    adj_load.start()

    def outside_rows(at):
        for ref in (ground, first, second, third):
            ref[pl.ds(at, DEPTH)] = jnp.full((DEPTH, SUBL, lanes), unreached, jnp.float32)

    pl.when(jnp.logical_not(has(-1)))(lambda: outside_rows(0))
    pl.when(jnp.logical_not(has(1)))(lambda: outside_rows(high))

    spans = {-1: (0, DEPTH), 0: (low, height), 1: (high, DEPTH)}
    for dc, ref in ((-1, ring_low), (1, ring_high)):
        for dr in (-1, 0, 1):

            def outside_ring(ref=ref, dr=dr):
                at, count = spans[dr]
                ref[:, pl.ds(at, count)] = jnp.full((2, count, 1, TILE), unreached, jnp.float32)

            pl.when(jnp.logical_not(both(dr, dc)))(outside_ring)

    adj_load.wait()
    lane_tile = lax.broadcasted_iota(jnp.int32, (n_tiles, padded), 1)
    linked = jnp.zeros((n_tiles, padded), jnp.float32)
    links = adj[...]
    for k in range(links.shape[1]):
        linked = jnp.where(links[:, k : k + 1] == lane_tile, 1.0, linked)
    own = lax.broadcasted_iota(jnp.int32, (n_tiles, padded), 0) == lane_tile
    linked = jnp.where(own, 1.0, linked)
    one_hop = linked
    if n_tiles < padded:
        one_hop = jnp.concatenate(
            [one_hop, jnp.zeros((padded - n_tiles, padded), jnp.float32)], axis=0
        )
    count = jnp.where(own, 0.0, 1.0)
    reach = linked
    for step in range(ROUNDS):
        count = count + (1.0 - reach)
        if step < ROUNDS - 1:
            reach = jnp.dot(reach, one_hop, preferred_element_type=jnp.float32)
            reach = jnp.where(reach > 0.5, 1.0, 0.0)
    hops[...] = count

    sub_id = lax.broadcasted_iota(jnp.int32, (SUBL, TILE), 0)
    lane_id = lax.broadcasted_iota(jnp.int32, (SUBL, TILE), 1)
    first_cell = jnp.logical_and(sub_id == 0, lane_id == 0)
    last_cell = jnp.logical_and(sub_id == SUBL - 1, lane_id == TILE - 1)
    is_first_col = (col == 0).astype(jnp.int32)
    is_last_col = (col == n_cols - 1).astype(jnp.int32)
    top_mark = jnp.where(band == 0, 1, 2)
    bottom_mark = jnp.where(band == bands - 1, 1, 2)
    right_half = lane_id < HALF

    def ring_of(ref, r):
        left_tile = ref[r, :, 0:TILE]
        right_tile = ref[r, :, chunk - TILE : chunk]
        return jnp.where(
            right_half, pltpu.roll(left_tile, SUBL - 1, 0), pltpu.roll(right_tile, 1, 0)
        )

    side_load.wait()
    for load in loads:
        load.wait()

    def start_row(i):
        height_row = ground[low + i, :, 0:chunk]
        water = height_row + fill[i]
        if i == 0:
            water = jnp.where(edge[0] == top_mark, height_row, water)
        if i == height - 1:
            water = jnp.where(edge[1] == bottom_mark, height_row, water)
        first[low + i, :, 0:chunk] = water
        mark = jnp.where(first_cell, side[0, i] * is_first_col, 0) == 1
        first[low + i, :, 0:TILE] = jnp.where(
            mark, ground[low + i, :, 0:TILE], first[low + i, :, 0:TILE]
        )
        at = chunk - TILE
        mark = jnp.where(last_cell, side[1, i] * is_last_col, 0) == 1
        first[low + i, :, at:chunk] = jnp.where(
            mark, ground[low + i, :, at:chunk], first[low + i, :, at:chunk]
        )
        for number, ref in enumerate((first, ground)):
            ring = ring_of(ref, low + i)
            ring_own[number, i] = ring
            ref[low + i, :, chunk:lanes] = ring

    order = [i for i in range(height) if i < DEPTH or i >= height - DEPTH]
    order += [i for i in range(height) if i not in order]
    for i in order:
        start_row(i)

    pl.semaphore_wait(barrier, members - 1)

    copies = []

    def send(src, dst, dr, dc):
        number = len(copies)
        copy = pltpu.make_async_remote_copy(
            src_ref=src,
            dst_ref=dst,
            send_sem=send_sem.at[number],
            recv_sem=recv_sem.at[number],
            device_id=device(dr, dc),
            device_id_type=MESH,
        )
        pl.when(both(dr, dc))(copy.start)
        copies.append((copy, dr, dc))
        return copy, dr, dc

    def arrive(entry, mirrored):
        copy, dr, dc = entry
        pl.when(both(-dr, -dc) if mirrored else both(dr, dc))(copy.wait_recv)

    def rows_out(ref, dr, extent):
        src = jnp.where(dr < 0, low, high - DEPTH)
        dst = jnp.where(dr < 0, high, 0)
        return send(
            ref.at[pl.ds(src, DEPTH), :, pl.ds(0, extent)],
            ref.at[pl.ds(dst, DEPTH), :, pl.ds(0, extent)],
            dr, 0,
        )

    ring_in = []
    for dc in (-1, 1):
        for dr in (-1, 0, 1):
            at, count = {-1: (0, DEPTH), 0: (0, height), 1: (height - DEPTH, DEPTH)}[dr]
            to, _ = spans[-dr]
            target = ring_high if dc == -1 else ring_low
            part = SUBL - 1 if dc == -1 else 0
            ring_in.append(
                send(
                    ring_own.at[:, pl.ds(at, count), pl.ds(part, 1)],
                    target.at[:, pl.ds(to, count)],
                    dr, dc,
                )
            )
    sides = (near, far)
    row_in = [[rows_out(ref, dr, chunk) for ref in (first, ground)] for dr in sides]

    def relax_rows(src, dst, r, count):
        rows = [src[r - 1 + i] for i in range(count + 2)]
        for i in range(count):
            above, here, below = rows[i : i + 3]
            low3 = jnp.minimum(jnp.minimum(above, below), here)
            least = jnp.minimum(
                low3, jnp.minimum(pltpu.roll(low3, 1, 1), pltpu.roll(low3, lanes - 1, 1))
            )
            value = jnp.maximum(ground[r + i], jnp.minimum(here, least + rise_step))
            if dst is done:
                done[r + i - low] = value[:, 0:chunk]
            else:
                dst[r + i] = value

    def inner(chain):
        for k in range(1, DEPTH + 1):
            for r in range(low + k, high - k, 2):
                relax_rows(chain[k - 1], chain[k], r, 2)

    def outer(chain, dr):
        for k in range(1, DEPTH + 1):
            begin = jnp.where(dr < 0, k, high - k)
            for i in range(0, DEPTH, 2):
                relax_rows(chain[k - 1], chain[k], begin + i, 2)

    def finish_ring(at, count, own_rows):
        for i in range(count):
            r = at + i
            for number, ref in enumerate((first, ground)):
                ring = ring_own[number, i] if own_rows else ring_of(ref, r)
                from_high = jnp.broadcast_to(ring_high[number, r], (SUBL, TILE))
                from_low = jnp.broadcast_to(ring_low[number, r], (SUBL, TILE))
                ring = jnp.where(at_high, from_high, jnp.where(at_low, from_low, ring))
                ref[r, :, chunk:lanes] = ring

    at_high = jnp.logical_and(sub_id == SUBL - 1, right_half)
    at_low = jnp.logical_and(sub_id == 0, jnp.logical_not(right_half))

    for entry in ring_in:
        arrive(entry, True)
    finish_ring(low, height, True)
    chain = (first, ping, pong, ping, second)
    inner(chain)
    row_next = []
    for dr, entries in zip(sides, row_in):
        for entry in entries:
            arrive(entry, False)
        finish_ring(jnp.where(dr < 0, 0, high), DEPTH, False)
        outer(chain, dr)
        row_next.append(rows_out(second, dr, lanes))

    row_in = row_next
    chain = (second, ping, pong, ping, third)
    inner(chain)
    for dr, entry in zip(sides, row_in):
        arrive(entry, False)
        outer(chain, dr)

    first_tile = third[low, :, 0:TILE]
    last_tile = third[low, :, chunk - TILE : chunk]
    for i in range(1, height):
        first_tile = jnp.minimum(first_tile, third[low + i, :, 0:TILE])
        last_tile = jnp.minimum(last_tile, third[low + i, :, chunk - TILE : chunk])
    floor = jnp.minimum(
        jnp.where(first_cell, first_tile, unreached), jnp.where(last_cell, last_tile, unreached)
    )
    for i, counts in ((low, sub == 0), (high - 1, sub == n_sub - 1)):
        skip = jnp.where(counts, -unreached, unreached)
        for j in range(chunk // TILE):
            floor = jnp.minimum(
                floor, jnp.maximum(third[i, :, j * TILE : (j + 1) * TILE], skip)
            )
    floor = jnp.min(floor, axis=(0, 1), keepdims=True)
    tile_id = tile_row * n_cols + col
    mine[...] = jnp.where(
        lax.broadcasted_iota(jnp.int32, (1, padded), 1) == tile_id,
        jnp.broadcast_to(floor, (1, padded)),
        unreached,
    )

    def level_copy(step):
        return pltpu.make_async_remote_copy(
            src_ref=mine,
            dst_ref=gathered.at[members - 1 - step],
            send_sem=level_send,
            recv_sem=level_recv,
            device_id=member((me + step) % members),
            device_id_type=MESH,
        )

    def spread(step, carry):
        level_copy(step).start()
        return carry

    lax.fori_loop(1, members, spread, 0)
    row_in = [rows_out(third, dr, lanes) for dr in (far, near)][::-1]

    chain = (third, ping, pong, ping, done)
    inner(chain)
    for dr, entry in zip(sides, row_in):
        arrive(entry, False)
        outer(chain, dr)

    def seam_of(ref, r):
        ring = ref[r, :, chunk:lanes]
        at_first = jnp.where(right_half, ref[r, :, 0:TILE], ring)
        at_last = jnp.where(right_half, ring, ref[r, :, chunk - TILE : chunk])
        return jnp.where(sub_id == 0, at_first, at_last)

    for r in range(total):
        seam_ground[r] = seam_of(ground, r)

    pltpu.make_async_copy(gathered, gathered, level_recv).wait()
    row = jnp.minimum(mine[...], jnp.min(gathered[...], axis=0))
    count = hops[...]
    best = jnp.full((n_tiles, padded), unreached, jnp.float32)
    for step in range(ROUNDS + 1):
        best = jnp.minimum(
            best, jnp.where(count == float(step), jnp.broadcast_to(row, best.shape), unreached)
        )
        row = row + hop_rise
    level = jnp.min(best, axis=1, keepdims=True)
    levels[...] = jnp.broadcast_to(level + spill_lift, levels.shape)

    def ceiling(row_at, col_at):
        at = jnp.clip(row_at, 0, n_rows - 1) * n_cols + jnp.clip(col_at, 0, n_cols - 1)
        return jnp.broadcast_to(levels[pl.ds(at, 1)], (SUBL, TILE))

    def ceilings(row_at):
        here = ceiling(row_at, col)
        beside = jnp.where(
            at_high, ceiling(row_at, col + 1), jnp.where(at_low, ceiling(row_at, col - 1), here)
        )
        return here, beside

    above, own_row, below = (ceilings((band + dr + n_sub) // n_sub - 1) for dr in (-1, 0, 1))
    beyond = ceilings((band + far + n_sub) // n_sub - 1)

    seam = []
    for r in range(total):
        top = (above if r < low else own_row if r < high else below)[1]
        seam.append(jnp.maximum(seam_ground[r], top))
    for k in range(1, DEPTH + 1):
        later = list(seam)
        for r in range(k, total - k):
            low3 = jnp.minimum(jnp.minimum(seam[r - 1], seam[r + 1]), seam[r])
            least = jnp.minimum(
                low3, jnp.minimum(pltpu.roll(low3, 1, 1), pltpu.roll(low3, TILE - 1, 1))
            )
            later[r] = jnp.maximum(seam_ground[r], jnp.minimum(seam[r], least + rise_step))
        seam = later
    for i in range(height):
        seam_ground[low + i] = seam[low + i]

    def flat(at, count, tops, targets):
        here, beside = tops
        for i in range(count):
            for j in range(lanes // TILE):
                cut = slice(j * TILE, (j + 1) * TILE)
                top = beside if j == lanes // TILE - 1 else here
                value = jnp.maximum(ground[at + i, :, cut], top)
                for target in targets:
                    target[at + i, :, cut] = value

    flat(jnp.where(far < 0, 0, high), DEPTH, beyond, (even,))
    flat(jnp.where(far < 0, low, high - DEPTH - 1), DEPTH + 1, own_row, (even, odd))
    outer((even, odd, even, odd, even), far)

    left_seam = jnp.logical_and(sub_id == 0, lane_id < DEPTH)
    right_seam = jnp.logical_and(sub_id == SUBL - 1, lane_id >= TILE - DEPTH)

    def merge(at, count, is_far):
        for i in range(count):
            r = at + i
            for j in range(chunk // TILE):
                cut = slice(j * TILE, (j + 1) * TILE)
                top = even[r, :, cut] if is_far else jnp.maximum(ground[r, :, cut], own_row[0])
                value = jnp.minimum(done[r - low, :, cut], top)
                if j == 0:
                    value = jnp.where(left_seam, jnp.minimum(value, seam_ground[r]), value)
                if j == chunk // TILE - 1:
                    value = jnp.where(right_seam, jnp.minimum(value, seam_ground[r]), value)
                done[r - low, :, cut] = value

    merge(jnp.where(far < 0, low + DEPTH, low), height - DEPTH, False)
    merge(jnp.where(far < 0, low, high - DEPTH), DEPTH, True)

    for s in range(SUBL):
        pltpu.make_async_copy(
            done.at[:, s], out_hbm.at[:, pl.ds(s * chunk, chunk)], out_sem
        ).start()
    for copy, dr, dc in copies:
        pl.when(both(dr, dc))(copy.wait_send)
    pltpu.make_async_copy(gathered, gathered, level_send).wait()
    pltpu.make_async_copy(done, done, out_sem).wait()


def per_device(sizes, elevation, fill_depth, edge_rows, edge_sides, adjacency):
    height, width = elevation.shape
    chunk = width // SUBL
    total = height + 2 * DEPTH
    members = sizes[1] * sizes[2] * sizes[3]
    n_tiles = adjacency.shape[0]
    padded = -(-n_tiles // TILE) * TILE
    wide = pltpu.VMEM((total, SUBL, chunk + TILE), jnp.float32)
    own = pltpu.VMEM((height, SUBL, chunk), jnp.float32)
    ring = pltpu.VMEM((2, total, 1, TILE), jnp.float32)
    return pl.pallas_call(
        functools.partial(kernel, sizes),
        out_shape=jax.ShapeDtypeStruct((height, width), jnp.float32),
        in_specs=[pl.BlockSpec(memory_space=pltpu.HBM)] * 5,
        out_specs=pl.BlockSpec(memory_space=pl.ANY),
        scratch_shapes=[
            wide, own, wide, wide, wide, wide, wide, own,
            pltpu.VMEM((2, SUBL, chunk), jnp.int32),
            pltpu.SMEM(edge_sides.shape, jnp.int32),
            pltpu.VMEM(adjacency.shape, jnp.int32),
            pltpu.VMEM((2, height, SUBL, TILE), jnp.float32),
            ring, ring,
            pltpu.VMEM((1, padded), jnp.float32),
            pltpu.VMEM((members - 1, 1, padded), jnp.float32),
            pltpu.VMEM((n_tiles, padded), jnp.float32),
            pltpu.VMEM((n_tiles, TILE), jnp.float32),
            wide, wide,
            pltpu.VMEM((total, SUBL, TILE), jnp.float32),
            pltpu.SemaphoreType.DMA((5,)),
            pltpu.SemaphoreType.DMA((14,)),
            pltpu.SemaphoreType.DMA((14,)),
            pltpu.SemaphoreType.DMA,
            pltpu.SemaphoreType.DMA,
            pltpu.SemaphoreType.DMA,
        ],
        compiler_params=pltpu.CompilerParams(
            collective_id=0, has_side_effects=True, vmem_limit_bytes=66 * 1000 * 1000
        ),
    )(elevation, fill_depth, edge_rows, edge_sides, adjacency)


def solution(mesh):
    sizes = tuple(mesh.shape[name] for name in ("groups", "rows", "cols", "sub"))
    placed = (
        P(("groups", "rows", "sub"), "cols"),
        P(("groups", "rows", "sub"), "cols"),
        P("groups", "cols"),
        P("groups", ("rows", "sub")),
        P("groups", None),
    )
    return jax.shard_map(
        functools.partial(per_device, sizes),
        mesh=mesh,
        in_specs=placed,
        out_specs=P(("groups", "rows", "sub"), "cols"),
        check_vma=False,
    )
```

```python
import functools

import jax
import jax.numpy as jnp
from jax import lax
from jax.experimental import pallas as pl
from jax.experimental.pallas import tpu as pltpu
from jax.sharding import PartitionSpec as P

PASSES = 8
FINAL = 4
ROUNDS = 4

unreached = 1000000000.0
rise_step = 0.01
hop_rise = 0.05
spill_lift = 3.0

DEEP = PASSES + FINAL
CUTS = (0, 4, 6, 8, 10, 12)
SUBL = 8
TILE = 128
HALF = TILE // 2
MESH = pl.DeviceIdType.MESH


def kernel(
    sizes, elev_hbm, fill_hbm, edge_hbm, side_hbm, adj_hbm, out,
    elev, fill, far_elev, ground, first, ping, pong, walks,
    edge, side, adj, ring_own, ring_low, ring_high, column_floor,
    mine, gathered, hops, levels, seam_ground,
    load_sem, send_sem, recv_sem, level_send, level_recv,
):
    n_groups, n_rows, n_cols, n_sub = sizes
    tiles = edge_hbm.shape[0] // (2 * SUBL)
    chunk = tiles * TILE
    lanes = chunk + TILE
    half_rows = SUBL * tiles * SUBL
    halves = elev_hbm.shape[0] // half_rows
    height = halves * SUBL
    n_tiles = adj.shape[0]
    padded = mine.shape[1]
    members = n_rows * n_cols * n_sub

    group = lax.axis_index("groups")
    tile_row = lax.axis_index("rows")
    col = lax.axis_index("cols")
    sub = lax.axis_index("sub")
    band = tile_row * n_sub + sub
    bands = n_rows * n_sub
    me = (tile_row * n_cols + col) * n_sub + sub

    near = 1 - 2 * sub
    far = -near

    def row_of(i):
        return jnp.where(sub == 0, i, height - 1 - i)

    def slot(i):
        if i < 0:
            return -1 - i
        if i < height:
            return DEEP + i
        return 2 * DEEP + 2 * height - 1 - i

    def has(dr):
        return jnp.logical_and(band + dr >= 0, band + dr < bands)

    has_col = {-1: col > 0, 1: col < n_cols - 1}

    def both(side_of, dc):
        there = {0: None, 1: has(far), 2: None}[side_of]
        if dc == 0:
            return there
        return has_col[dc] if there is None else jnp.logical_and(there, has_col[dc])

    def device(side_of, dc):
        to_band = band + {0: 0, 1: far, 2: near}[side_of]
        return (group, to_band // n_sub, col + dc, to_band % n_sub)

    def when(condition, action):
        if condition is None:
            action()
        else:
            pl.when(condition)(action)

    barrier = pltpu.get_barrier_semaphore()

    def member(number):
        return (group, number // (n_sub * n_cols), (number // n_sub) % n_cols, number % n_sub)

    def greet(step, carry):
        pl.semaphore_signal(
            barrier, inc=1, device_id=member((me + step) % members), device_id_type=MESH
        )
        return carry

    loads = []
    for part in range(halves):
        half = row_of(part * SUBL) // SUBL
        at = pl.ds(pl.multiple_of(half * half_rows, half_rows), half_rows)
        pair = []
        for number, (src, dst) in enumerate(((elev_hbm, elev), (fill_hbm, fill))):
            copy = pltpu.make_async_copy(src.at[at], dst.at[at], load_sem.at[2 * part + number])
            copy.start()
            pair.append(copy)
        loads.append(pair)
    spare = 2 * halves
    side_load = pltpu.make_async_copy(side_hbm, side, load_sem.at[spare])
    side_load.start()
    edge_load = pltpu.make_async_copy(edge_hbm, edge, load_sem.at[spare + 1])
    edge_load.start()
    adj_load = pltpu.make_async_copy(adj_hbm, adj, load_sem.at[spare + 2])
    adj_load.start()
    lax.fori_loop(1, members, greet, 0)

    def outside_rows():
        for ref in (ground, first):
            ref[0:DEEP] = jnp.full((DEEP, SUBL, lanes), unreached, jnp.float32)
        far_elev[...] = jnp.full(far_elev.shape, unreached, jnp.float32)

    pl.when(jnp.logical_not(has(far)))(outside_rows)

    spans = {0: (DEEP, height), 1: (0, DEEP), 2: (DEEP + height, DEEP)}
    for dc, ref in ((-1, ring_low), (1, ring_high)):
        for side_of in (0, 1, 2):

            def outside_ring(ref=ref, side_of=side_of):
                at, count = spans[side_of]
                ref[:, at : at + count] = jnp.full((2, count, 1, TILE), unreached, jnp.float32)

            pl.when(jnp.logical_not(both(side_of, dc)))(outside_ring)
    column_floor[...] = jnp.full(column_floor.shape, unreached, jnp.float32)

    sub_id = lax.broadcasted_iota(jnp.int32, (SUBL, TILE), 0)
    lane_id = lax.broadcasted_iota(jnp.int32, (SUBL, TILE), 1)
    first_cell = jnp.logical_and(sub_id == 0, lane_id == 0)
    last_cell = jnp.logical_and(sub_id == SUBL - 1, lane_id == TILE - 1)
    is_first_col = (col == 0).astype(jnp.int32)
    is_last_col = (col == n_cols - 1).astype(jnp.int32)
    at_slab_edge = jnp.where(has(far), 2, 1)
    right_half = lane_id < HALF
    at_high = jnp.logical_and(sub_id == SUBL - 1, right_half)
    at_low = jnp.logical_and(sub_id == 0, jnp.logical_not(right_half))

    def ring_of(ref, at):
        left_tile = ref[at, :, 0:TILE]
        right_tile = ref[at, :, chunk - TILE : chunk]
        return jnp.where(
            right_half, pltpu.roll(left_tile, SUBL - 1, 0), pltpu.roll(right_tile, 1, 0)
        )

    def piece(i, v):
        row = row_of(i)
        at = (row // SUBL) * half_rows + v * SUBL + row % SUBL
        return pl.ds(at, SUBL, stride=tiles * SUBL), slice(None)

    edge_side = jnp.where(far < 0, 0, 1)

    def start_row(i, columns):
        row = row_of(i)
        for v in columns:
            cut = slice(v * TILE, (v + 1) * TILE)
            here = elev[piece(i, v)]
            water = here + fill[piece(i, v)]
            if i == 0:
                marks = edge[pl.ds(2 * v + edge_side, SUBL, stride=2 * tiles), :]
                water = jnp.where(marks == at_slab_edge, here, water)
            if v == 0:
                mark = jnp.where(first_cell, side[0, row] * is_first_col, 0) == 1
                water = jnp.where(mark, here, water)
            if v == tiles - 1:
                mark = jnp.where(last_cell, side[1, row] * is_last_col, 0) == 1
                water = jnp.where(mark, here, water)
            ground[slot(i), :, cut] = here
            first[slot(i), :, cut] = water

    def start_ring(i):
        for number, ref in enumerate((first, ground)):
            ring_own[number, i] = ring_of(ref, slot(i))

    copies = []

    def send(src, dst, side_of, dc):
        number = len(copies)
        copy = pltpu.make_async_remote_copy(
            src_ref=src,
            dst_ref=dst,
            send_sem=send_sem.at[number],
            recv_sem=recv_sem.at[number],
            device_id=device(side_of, dc),
            device_id_type=MESH,
        )
        when(both(side_of, dc), copy.start)
        copies.append((copy, side_of, dc))
        return copy, side_of, dc

    def arrive(entry):
        copy, side_of, dc = entry
        when(both(side_of, -dc), copy.wait_recv)

    def send_rows(ref, side_of, i, count, to):
        return send(
            ref.at[pl.ds(slot(i), count), :, pl.ds(0, chunk)],
            ref.at[pl.ds(to, count), :, pl.ds(0, chunk)],
            side_of, 0,
        )

    def send_ring(side_of, i, count, to):
        sent = []
        for dc in (-1, 1):
            target = ring_high if dc == -1 else ring_low
            part = SUBL - 1 if dc == -1 else 0
            sent.append(
                send(
                    ring_own.at[:, pl.ds(i, count), pl.ds(part, 1)],
                    target.at[:, pl.ds(to, count)],
                    side_of, dc,
                )
            )
        return sent

    pl.semaphore_wait(barrier, members - 1)
    far_half = row_of(0) // SUBL
    at = pl.ds(pl.multiple_of(far_half * half_rows, half_rows), half_rows)
    far_ground = send(elev_hbm.at[at], far_elev, 1, 0)
    side_load.wait()
    edge_load.wait()
    for pair in loads:
        for load in pair:
            load.wait()
    for i in range(height):
        start_row(i, (0, tiles - 1))
        start_ring(i)
    own_ring = send_ring(0, 0, height, DEEP)
    near_ring = send_ring(2, height - DEEP, DEEP, DEEP + height)
    far_ring = send_ring(1, 0, DEEP, 0)
    between = range(1, tiles - 1)
    far_rows = []
    for begin, end in zip(CUTS[:-1], CUTS[1:]):
        for i in range(begin, end):
            if not SUBL + 2 <= i < DEEP - 1:
                start_row(i, between)
        entries = []
        if begin == SUBL:
            for i in range(end, DEEP - 1):
                start_row(i, between)
            entries.append(send_rows(ground, 1, SUBL, DEEP - 1 - SUBL, SUBL))
        entries.append(send_rows(first, 1, begin, end - begin, begin))
        far_rows.append(entries)
    far_rows[0].append(far_ground)
    for i in range(DEEP, height):
        start_row(i, between)
    near_rows = [
        send_rows(ref, 2, height - DEEP, DEEP, DEEP + height) for ref in (first, ground)
    ]

    adj_load.wait()
    lane_tile = lax.broadcasted_iota(jnp.int32, (n_tiles, padded), 1)
    linked = jnp.zeros((n_tiles, padded), jnp.float32)
    links = adj[...]
    for k in range(links.shape[1]):
        linked = jnp.where(links[:, k : k + 1] == lane_tile, 1.0, linked)
    own = lax.broadcasted_iota(jnp.int32, (n_tiles, padded), 0) == lane_tile
    linked = jnp.where(own, 1.0, linked)
    one_hop = linked
    if n_tiles < padded:
        one_hop = jnp.concatenate(
            [one_hop, jnp.zeros((padded - n_tiles, padded), jnp.float32)], axis=0
        )
    count = jnp.where(own, 0.0, 1.0)
    reach = linked
    for step in range(ROUNDS):
        count = count + (1.0 - reach)
        if step < ROUNDS - 1:
            reach = jnp.dot(reach, one_hop, preferred_element_type=jnp.float32)
            reach = jnp.where(reach > 0.5, 1.0, 0.0)
    hops[...] = count

    def finish_ring(i, own_row):
        at = slot(i)
        for number, ref in enumerate((first, ground)):
            ring = ring_own[number, i] if own_row else ring_of(ref, at)
            from_high = jnp.broadcast_to(ring_high[number, at], (SUBL, TILE))
            from_low = jnp.broadcast_to(ring_low[number, at], (SUBL, TILE))
            ring = jnp.where(at_high, from_high, jnp.where(at_low, from_low, ring))
            ref[at, :, chunk:lanes] = ring

    def state(k):
        return first if k == 0 else ping if k % 2 else pong

    def least_of(low):
        return jnp.minimum(
            low, jnp.minimum(pltpu.roll(low, 1, 1), pltpu.roll(low, lanes - 1, 1))
        )

    def relax(k, begin, end):
        src, dst = state(k - 1), state(k)
        for at in range(begin, end, 2):
            count = min(2, end - at)
            rows = [src[slot(at - 1 + j)] for j in range(count + 2)]
            for j in range(count):
                above, here, below = rows[j : j + 3]
                least = least_of(jnp.minimum(jnp.minimum(above, below), here))
                value = jnp.maximum(ground[slot(at + j)], jnp.minimum(here, least + rise_step))
                dst[slot(at + j)] = value
                if k == PASSES and 0 <= at + j < height:
                    column_floor[0] = jnp.minimum(column_floor[0], value[:, 0:TILE])
                    column_floor[1] = jnp.minimum(column_floor[1], value[:, chunk - TILE : chunk])

    for entry in own_ring:
        arrive(entry)
    for i in range(height):
        finish_ring(i, True)
    for k in range(1, height // 2):
        relax(k, k, height - k)

    for entry in near_rows + near_ring:
        arrive(entry)
    for i in range(height, height + DEEP):
        finish_ring(i, False)
    for k in range(1, PASSES + 1):
        relax(k, height - k, height + PASSES - k)

    def strip(number, passes):
        for k in passes:
            relax(k, k - CUTS[number + 1], k - CUTS[number])

    def open_strip(number):
        for entry in far_rows[number]:
            arrive(entry)
        for i in range(-CUTS[number + 1], -CUTS[number]):
            finish_ring(i, False)

    for entry in far_ring + far_rows[0]:
        arrive(entry)
    for i in range(SUBL):
        at = jnp.where(sub == 0, SUBL - 1 - i, i)
        for v in range(tiles):
            ground[slot(-1 - i), :, v * TILE : (v + 1) * TILE] = far_elev[
                pl.ds(at + v * SUBL, SUBL, stride=tiles * SUBL), :
            ]
    for i in range(-CUTS[1], 0):
        finish_ring(i, False)
    strip(0, range(1, PASSES + 1))
    for k in range(1, DEEP + 1):
        relax(k, k if k > PASSES else height + PASSES - k, height + DEEP - k)
    for number in (1, 2):
        open_strip(number)
        strip(number, range(1, PASSES + 1))

    floor = jnp.minimum(
        jnp.where(first_cell, column_floor[0], unreached),
        jnp.where(last_cell, column_floor[1], unreached),
    )
    for v in range(tiles):
        floor = jnp.minimum(floor, state(PASSES)[slot(0), :, v * TILE : (v + 1) * TILE])
    floor = jnp.min(floor, axis=(0, 1), keepdims=True)
    tile_id = tile_row * n_cols + col
    mine[...] = jnp.where(
        lax.broadcasted_iota(jnp.int32, (1, padded), 1) == tile_id,
        jnp.broadcast_to(floor, (1, padded)),
        unreached,
    )

    def level_copy(step):
        return pltpu.make_async_remote_copy(
            src_ref=mine,
            dst_ref=gathered.at[members - 1 - step],
            send_sem=level_send,
            recv_sem=level_recv,
            device_id=member((me + step) % members),
            device_id_type=MESH,
        )

    def spread(step, carry):
        level_copy(step).start()
        return carry

    lax.fori_loop(1, members, spread, 0)

    for k in range(PASSES + 1, DEEP + 1):
        relax(k, k - PASSES, k)

    def walk_at(n, r):
        return n * (n - 1) // 2 + r

    entry_row = ground[slot(-1)]
    entry_ring = jnp.where(jnp.logical_or(at_high, at_low), unreached, entry_row[:, chunk:lanes])
    before = [jnp.concatenate([entry_row[:, 0:chunk], entry_ring], axis=1)]
    for n in range(1, FINAL + 1):
        for r in range(n):
            low = None
            for q in range(max(r - 1, 0), min(r + 2, len(before))):
                row = before[q]
                low = row if low is None else jnp.minimum(low, row)
            walks[walk_at(n, r)] = jnp.maximum(ground[slot(r)], least_of(low) + rise_step)
        before = [walks[walk_at(n, r)] for r in range(n)]

    def seam_of(ref, at):
        ring = ref[at, :, chunk:lanes]
        at_first = jnp.where(right_half, ref[at, :, 0:TILE], ring)
        at_last = jnp.where(right_half, ring, ref[at, :, chunk - TILE : chunk])
        return jnp.where(sub_id == 0, at_first, at_last)

    seam_rows = list(range(-FINAL, height + FINAL))
    for j, i in enumerate(seam_rows):
        seam_ground[j] = seam_of(ground, slot(i))

    for number in (3, 4):
        open_strip(number)
        strip(number, range(1, DEEP + 1))

    pltpu.make_async_copy(gathered, gathered, level_recv).wait()
    row = jnp.minimum(mine[...], jnp.min(gathered[...], axis=0))
    count = hops[...]
    best = jnp.full((n_tiles, padded), unreached, jnp.float32)
    for step in range(ROUNDS + 1):
        best = jnp.minimum(
            best, jnp.where(count == float(step), jnp.broadcast_to(row, best.shape), unreached)
        )
        row = row + hop_rise
    level = jnp.min(best, axis=1, keepdims=True)
    levels[...] = jnp.broadcast_to(level + spill_lift, levels.shape)

    def ceiling(row_at, col_at):
        at = jnp.clip(row_at, 0, n_rows - 1) * n_cols + jnp.clip(col_at, 0, n_cols - 1)
        return jnp.broadcast_to(levels[pl.ds(at, 1)], (SUBL, TILE))

    def ceilings(row_at):
        here = ceiling(row_at, col)
        beside = jnp.where(
            at_high, ceiling(row_at, col + 1), jnp.where(at_low, ceiling(row_at, col - 1), here)
        )
        return here, beside

    own_top, own_beside = ceilings(tile_row)
    far_top, far_beside = ceilings(tile_row + far)

    seam = []
    for j, i in enumerate(seam_rows):
        seam.append(jnp.maximum(seam_ground[j], far_beside if i < 0 else own_beside))
    for k in range(1, FINAL + 1):
        later = list(seam)
        for j in range(k, len(seam) - k):
            low = jnp.minimum(jnp.minimum(seam[j - 1], seam[j + 1]), seam[j])
            least = jnp.minimum(low, jnp.minimum(pltpu.roll(low, 1, 1), pltpu.roll(low, TILE - 1, 1)))
            later[j] = jnp.maximum(seam_ground[j], jnp.minimum(seam[j], least + rise_step))
        seam = later

    left_seam = jnp.logical_and(sub_id == 0, lane_id < FINAL)
    right_seam = jnp.logical_and(sub_id == SUBL - 1, lane_id >= TILE - FINAL)
    tops = []
    for n in range(1, FINAL + 1):
        far_top = far_top + rise_step
        tops.append(far_top)
    for i in range(height):
        for v in range(tiles):
            cut = slice(v * TILE, (v + 1) * TILE)
            top = jnp.maximum(ground[slot(i), :, cut], own_top)
            for n in range(i + 1, FINAL + 1):
                top = jnp.minimum(top, jnp.maximum(walks[walk_at(n, i), :, cut], tops[n - 1]))
            value = jnp.minimum(state(DEEP)[slot(i), :, cut], top)
            if v == 0:
                value = jnp.where(left_seam, jnp.minimum(value, seam[i + FINAL]), value)
            if v == tiles - 1:
                value = jnp.where(right_seam, jnp.minimum(value, seam[i + FINAL]), value)
            out[piece(i, v)] = value

    for copy, side_of, dc in copies:
        when(both(side_of, dc), copy.wait_send)
    pltpu.make_async_copy(gathered, gathered, level_send).wait()


def per_device(sizes, elevation, fill_depth, edge_rows, edge_sides, adjacency):
    height, width = elevation.shape
    chunk = width // SUBL
    tiles = width // TILE
    total = height + 2 * DEEP
    members = sizes[1] * sizes[2] * sizes[3]
    n_tiles = adjacency.shape[0]
    padded = -(-n_tiles // TILE) * TILE
    flat = (height * tiles, TILE)

    def tiled(array):
        blocks = array.reshape(height // SUBL, SUBL, tiles, TILE)
        return blocks.transpose(0, 2, 1, 3).reshape(flat)

    wide = pltpu.VMEM((total, SUBL, chunk + TILE), jnp.float32)
    whole = pltpu.VMEM(flat, jnp.float32)
    ring = pltpu.VMEM((2, total, 1, TILE), jnp.float32)
    marks = edge_rows.reshape(2, tiles, TILE).transpose(1, 0, 2).reshape(2 * tiles, TILE)
    operands = (tiled(elevation), tiled(fill_depth), marks, edge_sides, adjacency)
    filled = pl.pallas_call(
        functools.partial(kernel, sizes),
        out_shape=pltpu.VMEM(flat, jnp.float32),
        in_specs=[pl.BlockSpec(memory_space=pltpu.HBM)] * 5,
        out_specs=pl.BlockSpec(memory_space=pltpu.VMEM),
        scratch_shapes=[
            whole, whole,
            pltpu.VMEM((SUBL * tiles, TILE), jnp.float32),
            wide, wide, wide, wide,
            pltpu.VMEM((FINAL * (FINAL + 1) // 2, SUBL, chunk + TILE), jnp.float32),
            pltpu.VMEM((2 * tiles, TILE), jnp.int32),
            pltpu.SMEM(edge_sides.shape, jnp.int32),
            pltpu.VMEM(adjacency.shape, jnp.int32),
            pltpu.VMEM((2, height, SUBL, TILE), jnp.float32),
            ring, ring,
            pltpu.VMEM((2, SUBL, TILE), jnp.float32),
            pltpu.VMEM((1, padded), jnp.float32),
            pltpu.VMEM((members - 1, 1, padded), jnp.float32),
            pltpu.VMEM((n_tiles, padded), jnp.float32),
            pltpu.VMEM((n_tiles, TILE), jnp.float32),
            pltpu.VMEM((height + 2 * FINAL, SUBL, TILE), jnp.float32),
            pltpu.SemaphoreType.DMA((2 * (height // SUBL) + 3,)),
            pltpu.SemaphoreType.DMA((15,)),
            pltpu.SemaphoreType.DMA((15,)),
            pltpu.SemaphoreType.DMA,
            pltpu.SemaphoreType.DMA,
        ],
        compiler_params=pltpu.CompilerParams(
            collective_id=0, has_side_effects=True, vmem_limit_bytes=32 * 1024 * 1024
        ),
    )(*(pltpu.with_memory_space_constraint(each, pltpu.HBM) for each in operands))
    blocks = filled.reshape(height // SUBL, tiles, SUBL, TILE)
    return blocks.transpose(0, 2, 1, 3).reshape(height, width)


def solution(mesh):
    sizes = tuple(mesh.shape[name] for name in ("groups", "rows", "cols", "sub"))
    placed = (
        P(("groups", "rows", "sub"), "cols"),
        P(("groups", "rows", "sub"), "cols"),
        P("groups", "cols"),
        P("groups", ("rows", "sub")),
        P("groups", None),
    )
    return jax.shard_map(
        functools.partial(per_device, sizes),
        mesh=mesh,
        in_specs=placed,
        out_specs=P(("groups", "rows", "sub"), "cols"),
        check_vma=False,
    )
```

```python
import functools

import jax
import jax.numpy as jnp
from jax import lax
from jax.experimental import pallas as pl
from jax.experimental.pallas import tpu as pltpu
from jax.sharding import PartitionSpec as P

PASSES = 8
FINAL = 4
ROUNDS = 4

unreached = 1000000000.0
rise_step = 0.01
hop_rise = 0.05
spill_lift = 3.0

DEEP = PASSES + FINAL
CUTS = (0, 4, 6, 8, 10, 12)
SUBL = 8
TILE = 128
HALF = TILE // 2
MESH = pl.DeviceIdType.MESH


def kernel(
    sizes, elev_hbm, fill_hbm, edge_hbm, side_hbm, adj_hbm, out,
    elev, fill, far_elev, ground, first, ping, pong, walks,
    edge, side, adj, ring_own, ring_low, ring_high, column_floor,
    mine, gathered, hops, levels, seam_ground, seam_sides, split, join,
    load_sem, send_sem, recv_sem, level_send, level_recv,
):
    n_groups, n_rows, n_cols, n_sub = sizes
    tiles = edge_hbm.shape[0] // (2 * SUBL)
    chunk = tiles * TILE
    pairs = tiles // 2
    lanes = chunk + 2 * TILE
    half_rows = SUBL * tiles * SUBL
    halves = elev_hbm.shape[0] // half_rows
    height = halves * SUBL
    n_tiles = adj.shape[0]
    padded = mine.shape[1]
    members = n_rows * n_cols * n_sub

    group = lax.axis_index("groups")
    tile_row = lax.axis_index("rows")
    col = lax.axis_index("cols")
    sub = lax.axis_index("sub")
    band = tile_row * n_sub + sub
    bands = n_rows * n_sub
    me = (tile_row * n_cols + col) * n_sub + sub

    near = 1 - 2 * sub
    far = -near

    def row_of(i):
        return jnp.where(sub == 0, i, height - 1 - i)

    def slot(i):
        if i < 0:
            return -1 - i
        if i < height:
            return DEEP + i
        return 2 * DEEP + 2 * height - 1 - i

    def has(dr):
        return jnp.logical_and(band + dr >= 0, band + dr < bands)

    has_col = {-1: col > 0, 1: col < n_cols - 1}

    def both(side_of, dc):
        there = {0: None, 1: has(far), 2: None}[side_of]
        if dc == 0:
            return there
        return has_col[dc] if there is None else jnp.logical_and(there, has_col[dc])

    def device(side_of, dc):
        to_band = band + {0: 0, 1: far, 2: near}[side_of]
        return (group, to_band // n_sub, col + dc, to_band % n_sub)

    def when(condition, action):
        if condition is None:
            action()
        else:
            pl.when(condition)(action)

    barrier = pltpu.get_barrier_semaphore()

    def member(number):
        return (group, number // (n_sub * n_cols), (number // n_sub) % n_cols, number % n_sub)

    def greet(step, carry):
        apart = step
        pl.semaphore_signal(
            barrier, inc=1, device_id=member((me + apart) % members), device_id_type=MESH
        )
        return carry

    lax.fori_loop(1, members, greet, 0)
    loads = []
    for part in range(halves):
        half = row_of(part * SUBL) // SUBL
        at = pl.ds(pl.multiple_of(half * half_rows, half_rows), half_rows)
        pair = []
        for number, (src, dst) in enumerate(((elev_hbm, elev), (fill_hbm, fill))):
            copy = pltpu.make_async_copy(src.at[at], dst.at[at], load_sem.at[2 * part + number])
            copy.start()
            pair.append(copy)
        loads.append(pair)
    spare = 2 * halves
    side_load = pltpu.make_async_copy(side_hbm, side, load_sem.at[spare])
    side_load.start()
    edge_load = pltpu.make_async_copy(edge_hbm, edge, load_sem.at[spare + 1])
    edge_load.start()
    adj_load = pltpu.make_async_copy(adj_hbm, adj, load_sem.at[spare + 2])
    adj_load.start()

    def outside_rows():
        for ref in (ground, first):
            ref[0:DEEP] = jnp.full((DEEP, SUBL, lanes), unreached, jnp.float32)
        far_elev[...] = jnp.full(far_elev.shape, unreached, jnp.float32)

    pl.when(jnp.logical_not(has(far)))(outside_rows)

    spans = {0: (DEEP, height), 1: (0, DEEP), 2: (DEEP + height, DEEP)}
    for dc, ref in ((-1, ring_low), (1, ring_high)):
        for side_of in (0, 1, 2):

            def outside_ring(ref=ref, side_of=side_of):
                at, count = spans[side_of]
                ref[:, at : at + count] = jnp.full((4, count, 1, TILE), unreached, jnp.float32)

            pl.when(jnp.logical_not(both(side_of, dc)))(outside_ring)
    column_floor[...] = jnp.full(column_floor.shape, unreached, jnp.float32)

    sub_id = lax.broadcasted_iota(jnp.int32, (SUBL, TILE), 0)
    lane_id = lax.broadcasted_iota(jnp.int32, (SUBL, TILE), 1)
    first_cell = jnp.logical_and(sub_id == 0, lane_id == 0)
    last_cell = jnp.logical_and(sub_id == SUBL - 1, lane_id == TILE - 1)
    is_first_col = (col == 0).astype(jnp.int32)
    is_last_col = (col == n_cols - 1).astype(jnp.int32)
    at_slab_edge = jnp.where(has(far), 2, 1)
    right_half = lane_id < HALF
    at_high = jnp.logical_and(sub_id == SUBL - 1, right_half)
    at_low = jnp.logical_and(sub_id == 0, jnp.logical_not(right_half))

    near_id = lax.broadcasted_iota(jnp.int32, (2 * TILE, 2 * TILE), 0)
    pair_id = lax.broadcasted_iota(jnp.int32, (2 * TILE, 2 * TILE), 1)
    split[...] = (near_id == 2 * (pair_id % TILE) + pair_id // TILE).astype(jnp.bfloat16)
    join[...] = (pair_id == 2 * (near_id % TILE) + near_id // TILE).astype(jnp.bfloat16)

    def shuffled(blocks, order):
        whole = jnp.concatenate([jnp.concatenate(block, axis=1) for block in blocks], axis=0)
        total = None
        for term in range(3):
            part = whole.astype(jnp.bfloat16)
            whole = whole - part.astype(jnp.float32)
            moved = jnp.dot(part, order[...], preferred_element_type=jnp.float32)
            total = moved if total is None else total + moved
        return [
            (total[SUBL * b : SUBL * (b + 1), 0:TILE], total[SUBL * b : SUBL * (b + 1), TILE : 2 * TILE])
            for b in range(len(blocks))
        ]

    def tile_of(ref, at, v):
        return ref[at, :, v * TILE : (v + 1) * TILE]

    def put_tile(ref, at, v, value):
        ref[at, :, v * TILE : (v + 1) * TILE] = value

    def ring_of(ref, at, p):
        return jnp.where(
            right_half,
            pltpu.roll(tile_of(ref, at, p), SUBL - 1, 0),
            pltpu.roll(tile_of(ref, at, tiles - 2 + p), 1, 0),
        )

    def turned(rows):
        rows = list(rows)
        for step in (4, 2, 1):
            stays = sub_id % (2 * step) < step
            for at in range(SUBL):
                if at % (2 * step) < step:
                    one, two = rows[at], rows[at + step]
                    rows[at] = jnp.where(stays, one, pltpu.roll(two, step, 0))
                    rows[at + step] = jnp.where(stays, pltpu.roll(one, SUBL - step, 0), two)
        return rows

    def natural(half, s, v):
        at = half * half_rows + (s * tiles + v) * SUBL
        return slice(at, at + SUBL)

    def by_side(action):
        pl.when(sub == 0)(lambda: action(False))
        pl.when(sub == 1)(lambda: action(True))

    def start_rows(part, groups):
        def action(flip):
            half = halves - 1 - part if flip else part
            for g in groups:
                here, water = {}, {}
                for v in (2 * g, 2 * g + 1):
                    rock = [elev[natural(half, s, v), :] for s in range(SUBL)]
                    deep = [rock[s] + fill[natural(half, s, v), :] for s in range(SUBL)]
                    here[v], water[v] = turned(rock), turned(deep)
                    for r in range(SUBL):
                        row = half * SUBL + r
                        if row == (height - 1 if flip else 0):
                            marks = edge[pl.ds(2 * v + flip, SUBL, stride=2 * tiles), :]
                            water[v][r] = jnp.where(marks == at_slab_edge, here[v][r], water[v][r])
                        if v == 0:
                            mark = jnp.where(first_cell, side[0, row] * is_first_col, 0) == 1
                            water[v][r] = jnp.where(mark, here[v][r], water[v][r])
                        if v == tiles - 1:
                            mark = jnp.where(last_cell, side[1, row] * is_last_col, 0) == 1
                            water[v][r] = jnp.where(mark, here[v][r], water[v][r])
                for ref, array in ((ground, here), (first, water)):
                    moved = shuffled([(array[2 * g][r], array[2 * g + 1][r]) for r in range(SUBL)], split)
                    for r, pair in enumerate(moved):
                        row = half * SUBL + r
                        for p in (0, 1):
                            put_tile(ref, slot(height - 1 - row if flip else row), 2 * g + p, pair[p])

        by_side(action)

    def start_ring(i):
        for number, ref in enumerate((first, ground)):
            for p in (0, 1):
                ring_own[2 * number + p, i] = ring_of(ref, slot(i), p)

    copies = []

    def send(src, dst, side_of, dc):
        number = len(copies)
        copy = pltpu.make_async_remote_copy(
            src_ref=src,
            dst_ref=dst,
            send_sem=send_sem.at[number],
            recv_sem=recv_sem.at[number],
            device_id=device(side_of, dc),
            device_id_type=MESH,
        )
        when(both(side_of, dc), copy.start)
        copies.append((copy, side_of, dc))
        return copy, side_of, dc

    def arrive(entry):
        copy, side_of, dc = entry
        when(both(side_of, -dc), copy.wait_recv)

    def send_rows(ref, side_of, i, count, to):
        return send(
            ref.at[pl.ds(slot(i), count), :, pl.ds(0, chunk)],
            ref.at[pl.ds(to, count), :, pl.ds(0, chunk)],
            side_of, 0,
        )

    def send_ring(side_of, i, count, to):
        sent = []
        for dc in (-1, 1):
            target = ring_high if dc == -1 else ring_low
            part = SUBL - 1 if dc == -1 else 0
            sent.append(
                send(
                    ring_own.at[:, pl.ds(i, count), pl.ds(part, 1)],
                    target.at[:, pl.ds(to, count)],
                    side_of, dc,
                )
            )
        return sent

    pl.semaphore_wait(barrier, members - 1)
    far_half = row_of(0) // SUBL
    at = pl.ds(pl.multiple_of(far_half * half_rows, half_rows), half_rows)
    far_ground = send(elev_hbm.at[at], far_elev, 1, 0)
    side_load.wait()
    edge_load.wait()
    for pair in loads:
        for load in pair:
            load.wait()
    for part in range(halves):
        start_rows(part, (0, pairs - 1))
    for i in range(height):
        start_ring(i)
    own_ring = send_ring(0, 0, height, DEEP)
    near_ring = send_ring(2, height - DEEP, DEEP, DEEP + height)
    far_ring = send_ring(1, 0, DEEP, 0)
    far_rows = []
    for part in range(halves):
        start_rows(part, range(1, pairs - 1))
        for begin, end in zip(CUTS[:-1], CUTS[1:]):
            if begin // SUBL == part:
                entries = []
                if begin == SUBL:
                    entries.append(send_rows(ground, 1, SUBL, DEEP - 1 - SUBL, SUBL))
                entries.append(send_rows(first, 1, begin, end - begin, begin))
                far_rows.append(entries)
    near_rows = [
        send_rows(ref, 2, height - DEEP, DEEP, DEEP + height) for ref in (first, ground)
    ]

    adj_load.wait()
    lane_tile = lax.broadcasted_iota(jnp.int32, (n_tiles, padded), 1)
    linked = jnp.zeros((n_tiles, padded), jnp.float32)
    links = adj[...]
    for k in range(links.shape[1]):
        linked = jnp.where(links[:, k : k + 1] == lane_tile, 1.0, linked)
    own = lax.broadcasted_iota(jnp.int32, (n_tiles, padded), 0) == lane_tile
    linked = jnp.where(own, 1.0, linked)
    one_hop = linked
    if n_tiles < padded:
        one_hop = jnp.concatenate(
            [one_hop, jnp.zeros((padded - n_tiles, padded), jnp.float32)], axis=0
        )
    count = jnp.where(own, 0.0, 1.0)
    reach = linked
    for step in range(ROUNDS):
        count = count + (1.0 - reach)
        if step < ROUNDS - 1:
            reach = jnp.dot(reach, one_hop, preferred_element_type=jnp.float32)
            reach = jnp.where(reach > 0.5, 1.0, 0.0)
    hops[...] = count

    def finish_ring(i, own_row, only=None):
        at = slot(i)
        for number, ref in enumerate((first, ground)):
            if only is not None and ref is not only:
                continue
            for p in (0, 1):
                ring = ring_own[2 * number + p, i] if own_row else ring_of(ref, at, p)
                from_high = jnp.broadcast_to(ring_high[2 * number + p, at], (SUBL, TILE))
                from_low = jnp.broadcast_to(ring_low[2 * number + p, at], (SUBL, TILE))
                ring = jnp.where(at_high, from_high, jnp.where(at_low, from_low, ring))
                put_tile(ref, at, tiles + p, ring)

    def state(k):
        return first if k == 0 else ping if k % 2 else pong

    all_tiles = range(tiles + 2)
    lowest_lane = lane_id == 0
    highest_lane = lane_id == TILE - 1

    def row_tiles(ref, at):
        return [tile_of(ref, at, v) for v in all_tiles]

    def lower(*rows):
        return [functools.reduce(jnp.minimum, tiles_at) for tiles_at in zip(*rows)]

    def least_of(low):
        even, odd = low[0::2], low[1::2]
        count = len(even)
        up = [pltpu.roll(each, 1, 1) for each in odd]
        down = [pltpu.roll(each, TILE - 1, 1) for each in even]
        least = []
        for g in range(count):
            both_of = jnp.minimum(even[g], odd[g])
            before = up[g] if count == 1 else jnp.where(lowest_lane, up[g - 1], up[g])
            after = down[g] if count == 1 else jnp.where(highest_lane, down[(g + 1) % count], down[g])
            least += [jnp.minimum(both_of, before), jnp.minimum(both_of, after)]
        return least

    def relax(k, begin, end):
        src, dst = state(k - 1), state(k)
        for at in range(begin, end, 2):
            count = min(2, end - at)
            rows = [row_tiles(src, slot(at - 1 + j)) for j in range(count + 2)]
            for j in range(count):
                above, here, below = rows[j : j + 3]
                if count == 2:
                    middle = lower(rows[1], rows[2]) if j == 0 else middle
                    least = least_of(lower(middle, above if j == 0 else below))
                else:
                    least = least_of(lower(above, below, here))
                values = []
                for v in range(tiles if k == DEEP else tiles + 2):
                    rock = tile_of(ground, slot(at + j), v)
                    values.append(jnp.maximum(rock, jnp.minimum(here[v], least[v] + rise_step)))
                if k == DEEP:
                    finish_row(at + j, values)
                    continue
                for v, value in enumerate(values):
                    put_tile(dst, slot(at + j), v, value)
                if k == PASSES and 0 <= at + j < height:
                    column_floor[0] = jnp.minimum(column_floor[0], values[0])
                    column_floor[1] = jnp.minimum(column_floor[1], values[tiles - 1])

    def finish_row(i, values):
        if i >= FINAL:
            moved = shuffled([(values[2 * g], values[2 * g + 1]) for g in range(pairs)], join)
            values = [each for pair in moved for each in pair]
        for v, value in enumerate(values):
            put_tile(state(DEEP), slot(i), v, value)

    for entry in own_ring:
        arrive(entry)
    for i in range(height):
        finish_ring(i, True)
    for k in range(1, height // 2):
        relax(k, k, height - k)

    for entry in near_rows + near_ring:
        arrive(entry)
    for i in range(height, height + DEEP):
        finish_ring(i, False)
    for k in range(1, PASSES + 1):
        relax(k, height - k, height + PASSES - k)

    def strip(number, passes):
        for k in passes:
            relax(k, k - CUTS[number + 1], k - CUTS[number])

    def open_strip(number):
        for entry in far_rows[number]:
            arrive(entry)
        for i in range(-CUTS[number + 1], -CUTS[number]):
            finish_ring(i, False, first)
            if -DEEP < i < -SUBL:
                finish_ring(i, False, ground)

    for entry in far_ring + [far_ground]:
        arrive(entry)

    def far_start(flip):
        for g in range(pairs):
            rock = [turned([far_elev[natural(0, s, 2 * g + p), :] for s in range(SUBL)]) for p in (0, 1)]
            moved = shuffled(list(zip(*rock)), split)
            for r, pair in enumerate(moved):
                for p in (0, 1):
                    put_tile(ground, slot(-1 - (r if flip else SUBL - 1 - r)), 2 * g + p, pair[p])

    by_side(far_start)
    for i in range(-SUBL, 0):
        finish_ring(i, False, ground)

    for entry in far_rows[0]:
        arrive(entry)
    for i in range(-CUTS[1], 0):
        finish_ring(i, False, first)
    for k in range(1, PASSES + 1):
        strip(0, (k,))
        relax(k, height + PASSES - k, height + DEEP - k)
    for number in (1, 2):
        open_strip(number)
        strip(number, range(1, PASSES + 1))

    floor = jnp.minimum(
        jnp.where(first_cell, column_floor[0], unreached),
        jnp.where(last_cell, column_floor[1], unreached),
    )
    for v in range(tiles):
        floor = jnp.minimum(floor, tile_of(state(PASSES), slot(0), v))
    floor = jnp.min(floor, axis=(0, 1), keepdims=True)
    tile_id = tile_row * n_cols + col
    mine[...] = jnp.where(
        lax.broadcasted_iota(jnp.int32, (1, padded), 1) == tile_id,
        jnp.broadcast_to(floor, (1, padded)),
        unreached,
    )

    def level_copy(step):
        return pltpu.make_async_remote_copy(
            src_ref=mine,
            dst_ref=gathered.at[members - 1 - step],
            send_sem=level_send,
            recv_sem=level_recv,
            device_id=member((me + step) % members),
            device_id_type=MESH,
        )

    def spread(step, carry):
        level_copy(step).start()
        return carry

    lax.fori_loop(1, members, spread, 0)

    for k in range(PASSES + 1, DEEP + 1):
        relax(k, k - PASSES, height + DEEP - k)

    def walk_at(n, r):
        return n * (n - 1) // 2 + r

    outside_ring_cells = jnp.logical_or(at_high, at_low)
    entry_row = row_tiles(ground, slot(-1))
    for v in (tiles, tiles + 1):
        entry_row[v] = jnp.where(outside_ring_cells, unreached, entry_row[v])
    before = [entry_row]
    for n in range(1, FINAL + 1):
        after = []
        for r in range(n):
            least = least_of(lower(*before[max(r - 1, 0) : r + 2]))
            rock = row_tiles(ground, slot(r))
            after.append([jnp.maximum(rock[v], least[v] + rise_step) for v in all_tiles])
            for v in range(tiles):
                put_tile(walks, walk_at(n, r), v, after[r][v])
        before = after

    def seam_of(ref, at, p):
        ring = tile_of(ref, at, tiles + p)
        at_first = jnp.where(right_half, tile_of(ref, at, p), ring)
        at_last = jnp.where(right_half, ring, tile_of(ref, at, tiles - 2 + p))
        return jnp.where(sub_id == 0, at_first, at_last)

    seam_rows = list(range(-FINAL, height + FINAL))
    moved = shuffled([(seam_of(ground, slot(i), 0), seam_of(ground, slot(i), 1)) for i in seam_rows], join)
    for j, pair in enumerate(moved):
        seam_ground[j] = jnp.where(right_half, pair[0], pair[1])
    for number in (3, 4):
        open_strip(number)
        strip(number, range(1, DEEP + 1))

    pltpu.make_async_copy(gathered, gathered, level_recv).wait()
    row = jnp.minimum(mine[...], jnp.min(gathered[...], axis=0))
    count = hops[...]
    best = jnp.full((n_tiles, padded), unreached, jnp.float32)
    for step in range(ROUNDS + 1):
        best = jnp.minimum(
            best, jnp.where(count == float(step), jnp.broadcast_to(row, best.shape), unreached)
        )
        row = row + hop_rise
    level = jnp.min(best, axis=1, keepdims=True)
    levels[...] = jnp.broadcast_to(level + spill_lift, levels.shape)

    def ceiling(row_at, col_at):
        at = jnp.clip(row_at, 0, n_rows - 1) * n_cols + jnp.clip(col_at, 0, n_cols - 1)
        return jnp.broadcast_to(levels[pl.ds(at, 1)], (SUBL, TILE))

    def ceilings(row_at):
        here = ceiling(row_at, col)
        beside = jnp.where(
            at_high, ceiling(row_at, col + 1), jnp.where(at_low, ceiling(row_at, col - 1), here)
        )
        return here, beside

    own_top, own_beside = ceilings(tile_row)
    far_top, far_beside = ceilings(tile_row + far)

    seam = []
    for j, i in enumerate(seam_rows):
        seam.append(jnp.maximum(seam_ground[j], far_beside if i < 0 else own_beside))
    for k in range(1, FINAL + 1):
        later = list(seam)
        for j in range(k, len(seam) - k):
            low = jnp.minimum(jnp.minimum(seam[j - 1], seam[j + 1]), seam[j])
            least = jnp.minimum(low, jnp.minimum(pltpu.roll(low, 1, 1), pltpu.roll(low, TILE - 1, 1)))
            later[j] = jnp.maximum(seam_ground[j], jnp.minimum(seam[j], least + rise_step))
        seam = later

    for i in range(height):
        row = pl.ds(row_of(i), 1)
        seam_sides[0, row, :] = seam[i + FINAL][0:1]
        seam_sides[1, row, :] = seam[i + FINAL][SUBL - 1 : SUBL]
    tops = []
    for n in range(1, FINAL + 1):
        far_top = far_top + rise_step
        tops.append(far_top)
    blocks = []
    for i in range(FINAL):
        values = row_tiles(state(DEEP), slot(i))
        for v in range(tiles):
            for n in range(i + 1, FINAL + 1):
                walk = tile_of(walks, walk_at(n, i), v)
                values[v] = jnp.minimum(values[v], jnp.maximum(walk, tops[n - 1]))
        blocks += [(values[2 * g], values[2 * g + 1]) for g in range(pairs)]
    moved = shuffled(blocks, join)
    for i in range(FINAL):
        for v in range(tiles):
            put_tile(state(DEEP), slot(i), v, moved[i * pairs + v // 2][v % 2])

    def finish(flip):
        for half in (range(halves - 1, -1, -1) if not flip else range(halves)):
            for v in range(tiles):
                order = [half * SUBL + r for r in range(SUBL)]
                order = [height - 1 - row if flip else row for row in order]
                rows = turned([tile_of(state(DEEP), slot(i), v) for i in order])
                for s in range(SUBL):
                    at = natural(half, s, v)
                    value = jnp.minimum(rows[s], jnp.maximum(elev[at, :], own_top))
                    at_half = slice(half * SUBL, (half + 1) * SUBL)
                    if s == 0 and v == 0:
                        left = jnp.minimum(value, seam_sides[0, at_half, :])
                        value = jnp.where(lane_id < FINAL, left, value)
                    if s == SUBL - 1 and v == tiles - 1:
                        right = jnp.minimum(value, seam_sides[1, at_half, :])
                        value = jnp.where(lane_id >= TILE - FINAL, right, value)
                    out[at, :] = value

    by_side(finish)

    for copy, side_of, dc in copies:
        when(both(side_of, dc), copy.wait_send)
    pltpu.make_async_copy(gathered, gathered, level_send).wait()


def per_device(sizes, elevation, fill_depth, edge_rows, edge_sides, adjacency):
    height, width = elevation.shape
    chunk = width // SUBL
    tiles = width // TILE
    total = height + 2 * DEEP
    members = sizes[1] * sizes[2] * sizes[3]
    n_tiles = adjacency.shape[0]
    padded = -(-n_tiles // TILE) * TILE
    flat = (height * tiles, TILE)

    def tiled(array):
        blocks = array.reshape(height // SUBL, SUBL, tiles, TILE)
        return blocks.transpose(0, 2, 1, 3).reshape(flat)

    wide = pltpu.VMEM((total, SUBL, chunk + 2 * TILE), jnp.float32)
    shuffle = pltpu.VMEM((2 * TILE, 2 * TILE), jnp.bfloat16)
    whole = pltpu.VMEM(flat, jnp.float32)
    ring = pltpu.VMEM((4, total, 1, TILE), jnp.float32)
    marks = edge_rows.reshape(2, tiles, TILE).transpose(1, 0, 2).reshape(2 * tiles, TILE)
    operands = (tiled(elevation), tiled(fill_depth), marks, edge_sides, adjacency)
    filled = pl.pallas_call(
        functools.partial(kernel, sizes),
        out_shape=pltpu.VMEM(flat, jnp.float32),
        in_specs=[pl.BlockSpec(memory_space=pltpu.HBM)] * 5,
        out_specs=pl.BlockSpec(memory_space=pltpu.VMEM),
        scratch_shapes=[
            whole, whole,
            pltpu.VMEM((SUBL * tiles, TILE), jnp.float32),
            wide, wide, wide, wide,
            pltpu.VMEM((FINAL * (FINAL + 1) // 2, SUBL, chunk), jnp.float32),
            pltpu.VMEM((2 * tiles, TILE), jnp.int32),
            pltpu.SMEM(edge_sides.shape, jnp.int32),
            pltpu.VMEM(adjacency.shape, jnp.int32),
            pltpu.VMEM((4, height, SUBL, TILE), jnp.float32),
            ring, ring,
            pltpu.VMEM((2, SUBL, TILE), jnp.float32),
            pltpu.VMEM((1, padded), jnp.float32),
            pltpu.VMEM((members - 1, 1, padded), jnp.float32),
            pltpu.VMEM((n_tiles, padded), jnp.float32),
            pltpu.VMEM((n_tiles, TILE), jnp.float32),
            pltpu.VMEM((height + 2 * FINAL, SUBL, TILE), jnp.float32),
            pltpu.VMEM((2, height, TILE), jnp.float32),
            shuffle, shuffle,
            pltpu.SemaphoreType.DMA((2 * (height // SUBL) + 3,)),
            pltpu.SemaphoreType.DMA((15,)),
            pltpu.SemaphoreType.DMA((15,)),
            pltpu.SemaphoreType.DMA,
            pltpu.SemaphoreType.DMA,
        ],
        compiler_params=pltpu.CompilerParams(
            collective_id=0, has_side_effects=True, vmem_limit_bytes=32 * 1024 * 1024
        ),
    )(*(pltpu.with_memory_space_constraint(each, pltpu.HBM) for each in operands))
    blocks = filled.reshape(height // SUBL, tiles, SUBL, TILE)
    return blocks.transpose(0, 2, 1, 3).reshape(height, width)


def solution(mesh):
    sizes = tuple(mesh.shape[name] for name in ("groups", "rows", "cols", "sub"))
    placed = (
        P(("groups", "rows", "sub"), "cols"),
        P(("groups", "rows", "sub"), "cols"),
        P("groups", "cols"),
        P("groups", ("rows", "sub")),
        P("groups", None),
    )
    return jax.shard_map(
        functools.partial(per_device, sizes),
        mesh=mesh,
        in_specs=placed,
        out_specs=P(("groups", "rows", "sub"), "cols"),
        check_vma=False,
    )
```

```python
import functools

import jax
import jax.numpy as jnp
from jax import lax
from jax.experimental import pallas as pl
from jax.experimental.pallas import tpu as pltpu
from jax.sharding import PartitionSpec as P

PASSES = 8
FINAL = 4
ROUNDS = 4

unreached = 1000000000.0
rise_step = 0.01
hop_rise = 0.05
spill_lift = 3.0

DEEP = PASSES + FINAL
REACH = DEEP // 2
CUTS = (0, 4, REACH + 1, PASSES, PASSES + 2, DEEP)
SUBL = 8
TILE = 128
HALF = TILE // 2
MESH = pl.DeviceIdType.MESH


def kernel(
    sizes, elev_hbm, fill_hbm, edge_hbm, side_hbm, adj_hbm, out,
    elev, fill, far_elev, ground, first, ping, pong, walks, times_out, times_in,
    edge, side, adj, ring_own, ring_low, ring_high, column_floor,
    mine, gathered, hops, levels, seam_ground, seam_sides, split, join,
    load_sem, send_sem, recv_sem, level_send, level_recv,
):
    n_groups, n_rows, n_cols, n_sub = sizes
    tiles = edge_hbm.shape[0] // (2 * SUBL)
    chunk = tiles * TILE
    pairs = tiles // 2
    lanes = chunk + 2 * TILE
    half_tiles = tiles * SUBL
    half_rows = SUBL * half_tiles
    halves = elev_hbm.shape[0] // half_tiles
    height = halves * SUBL
    n_tiles = adj.shape[0]
    padded = mine.shape[1]
    members = n_rows * n_cols * n_sub

    group = lax.axis_index("groups")
    tile_row = lax.axis_index("rows")
    col = lax.axis_index("cols")
    sub = lax.axis_index("sub")
    band = tile_row * n_sub + sub
    bands = n_rows * n_sub
    me = (tile_row * n_cols + col) * n_sub + sub

    near = 1 - 2 * sub
    far = -near

    def row_of(i):
        return jnp.where(sub == 0, i, height - 1 - i)

    def slot(i):
        if i < 0:
            return -1 - i
        if i < height:
            return DEEP + i
        return 2 * DEEP + 2 * height - 1 - i

    def has(dr):
        return jnp.logical_and(band + dr >= 0, band + dr < bands)

    has_col = {-1: col > 0, 1: col < n_cols - 1}

    def both(side_of, dc):
        there = {0: None, 1: has(far), 2: None}[side_of]
        if dc == 0:
            return there
        return has_col[dc] if there is None else jnp.logical_and(there, has_col[dc])

    def device(side_of, dc):
        to_band = band + {0: 0, 1: far, 2: near}[side_of]
        return (group, to_band // n_sub, col + dc, to_band % n_sub)

    def when(condition, action):
        if condition is None:
            action()
        else:
            pl.when(condition)(action)

    barrier = pltpu.get_barrier_semaphore()

    def member(number):
        return (group, number // (n_sub * n_cols), (number // n_sub) % n_cols, number % n_sub)

    def greet(step, carry):
        apart = step
        pl.semaphore_signal(
            barrier, inc=1, device_id=member((me + apart) % members), device_id_type=MESH
        )
        return carry

    lax.fori_loop(1, members, greet, 0)
    loads = []
    for part in range(halves):
        half = row_of(part * SUBL) // SUBL
        at = pl.ds(half * half_tiles, half_tiles)
        pair = []
        for number, (src, dst) in enumerate(((elev_hbm, elev), (fill_hbm, fill))):
            copy = pltpu.make_async_copy(src.at[at], dst.at[at], load_sem.at[2 * part + number])
            copy.start()
            pair.append(copy)
        loads.append(pair)
    spare = 2 * halves
    side_load = pltpu.make_async_copy(side_hbm, side, load_sem.at[spare])
    side_load.start()
    edge_load = pltpu.make_async_copy(edge_hbm, edge, load_sem.at[spare + 1])
    edge_load.start()
    adj_load = pltpu.make_async_copy(adj_hbm, adj, load_sem.at[spare + 2])
    adj_load.start()

    def outside_rows():
        for ref in (ground, first):
            ref[0:DEEP] = jnp.full((DEEP, SUBL, lanes), unreached, jnp.float32)
        for ref in (far_elev, times_in):
            ref[...] = jnp.full(ref.shape, unreached, jnp.float32)

    pl.when(jnp.logical_not(has(far)))(outside_rows)

    spans = {0: (DEEP, height), 1: (0, DEEP), 2: (DEEP + height, DEEP)}
    for dc, ref in ((-1, ring_low), (1, ring_high)):
        for side_of in (0, 1, 2):

            def outside_ring(ref=ref, side_of=side_of):
                at, count = spans[side_of]
                ref[:, at : at + count] = jnp.full((4, count, 1, TILE), unreached, jnp.float32)

            pl.when(jnp.logical_not(both(side_of, dc)))(outside_ring)
    column_floor[...] = jnp.full(column_floor.shape, unreached, jnp.float32)

    sub_id = lax.broadcasted_iota(jnp.int32, (SUBL, TILE), 0)
    lane_id = lax.broadcasted_iota(jnp.int32, (SUBL, TILE), 1)
    first_cell = jnp.logical_and(sub_id == 0, lane_id == 0)
    last_cell = jnp.logical_and(sub_id == SUBL - 1, lane_id == TILE - 1)
    is_first_col = (col == 0).astype(jnp.int32)
    is_last_col = (col == n_cols - 1).astype(jnp.int32)
    at_slab_edge = jnp.where(has(far), 2, 1)
    right_half = lane_id < HALF
    at_high = jnp.logical_and(sub_id == SUBL - 1, right_half)
    at_low = jnp.logical_and(sub_id == 0, jnp.logical_not(right_half))

    near_id = lax.broadcasted_iota(jnp.int32, (2 * TILE, 2 * TILE), 0)
    pair_id = lax.broadcasted_iota(jnp.int32, (2 * TILE, 2 * TILE), 1)
    split[...] = (near_id == 2 * (pair_id % TILE) + pair_id // TILE).astype(jnp.bfloat16)
    join[...] = (pair_id == 2 * (near_id % TILE) + near_id // TILE).astype(jnp.bfloat16)

    def shuffled(blocks, order):
        whole = jnp.concatenate([jnp.concatenate(block, axis=1) for block in blocks], axis=0)
        total = None
        for term in range(3):
            part = whole.astype(jnp.bfloat16)
            whole = whole - part.astype(jnp.float32)
            moved = jnp.dot(part, order[...], preferred_element_type=jnp.float32)
            total = moved if total is None else total + moved
        return [
            (total[SUBL * b : SUBL * (b + 1), 0:TILE], total[SUBL * b : SUBL * (b + 1), TILE : 2 * TILE])
            for b in range(len(blocks))
        ]

    def tile_of(ref, at, v):
        return ref[at, :, v * TILE : (v + 1) * TILE]

    def put_tile(ref, at, v, value):
        ref[at, :, v * TILE : (v + 1) * TILE] = value

    def ring_of(ref, at, p):
        return jnp.where(
            right_half,
            pltpu.roll(tile_of(ref, at, p), SUBL - 1, 0),
            pltpu.roll(tile_of(ref, at, tiles - 2 + p), 1, 0),
        )

    def turned(rows):
        rows = list(rows)
        for step in (4, 2, 1):
            stays = sub_id % (2 * step) < step
            for at in range(SUBL):
                if at % (2 * step) < step:
                    one, two = rows[at], rows[at + step]
                    rows[at] = jnp.where(stays, one, pltpu.roll(two, step, 0))
                    rows[at + step] = jnp.where(stays, pltpu.roll(one, SUBL - step, 0), two)
        return rows

    def number_of(half, s, v):
        return half * half_tiles + s * tiles + v

    def by_side(action):
        pl.when(sub == 0)(lambda: action(False))
        pl.when(sub == 1)(lambda: action(True))

    def start_rows(part, groups):
        def action(flip):
            half = halves - 1 - part if flip else part
            for g in groups:
                here, water = {}, {}
                for v in (2 * g, 2 * g + 1):
                    rock = [elev[number_of(half, s, v)] for s in range(SUBL)]
                    deep = [rock[s] + fill[number_of(half, s, v)] for s in range(SUBL)]
                    here[v], water[v] = turned(rock), turned(deep)
                    for r in range(SUBL):
                        row = half * SUBL + r
                        if row == (height - 1 if flip else 0):
                            marks = edge[pl.ds(2 * v + flip, SUBL, stride=2 * tiles), :]
                            water[v][r] = jnp.where(marks == at_slab_edge, here[v][r], water[v][r])
                        if v == 0:
                            mark = jnp.where(first_cell, side[0, row] * is_first_col, 0) == 1
                            water[v][r] = jnp.where(mark, here[v][r], water[v][r])
                        if v == tiles - 1:
                            mark = jnp.where(last_cell, side[1, row] * is_last_col, 0) == 1
                            water[v][r] = jnp.where(mark, here[v][r], water[v][r])
                for ref, array in ((ground, here), (first, water)):
                    moved = shuffled([(array[2 * g][r], array[2 * g + 1][r]) for r in range(SUBL)], split)
                    for r, pair in enumerate(moved):
                        row = half * SUBL + r
                        for p in (0, 1):
                            put_tile(ref, slot(height - 1 - row if flip else row), 2 * g + p, pair[p])

        by_side(action)

    def start_ring(i):
        for number, ref in enumerate((first, ground)):
            for p in (0, 1):
                ring_own[2 * number + p, i] = ring_of(ref, slot(i), p)

    copies = []

    def send(src, dst, side_of, dc):
        number = len(copies)
        copy = pltpu.make_async_remote_copy(
            src_ref=src,
            dst_ref=dst,
            send_sem=send_sem.at[number],
            recv_sem=recv_sem.at[number],
            device_id=device(side_of, dc),
            device_id_type=MESH,
        )
        when(both(side_of, dc), copy.start)
        copies.append((copy, side_of, dc))
        return copy, side_of, dc

    def arrive(entry):
        copy, side_of, dc = entry
        when(both(side_of, -dc), copy.wait_recv)

    def send_rows(ref, side_of, i, count, to):
        return send(
            ref.at[pl.ds(slot(i), count), :, pl.ds(0, chunk)],
            ref.at[pl.ds(to, count), :, pl.ds(0, chunk)],
            side_of, 0,
        )

    def send_ring(side_of, i, count, to):
        sent = []
        for dc in (-1, 1):
            target = ring_high if dc == -1 else ring_low
            part = SUBL - 1 if dc == -1 else 0
            sent.append(
                send(
                    ring_own.at[:, pl.ds(i, count), pl.ds(part, 1)],
                    target.at[:, pl.ds(to, count)],
                    side_of, dc,
                )
            )
        return sent

    pl.semaphore_wait(barrier, members - 1)
    far_half = pl.ds((row_of(0) // SUBL) * half_tiles, half_tiles)
    far_cut = pl.ds(jnp.where(sub == 0, 0, SUBL - REACH), REACH)
    far_ground = send(elev_hbm.at[far_half, far_cut], far_elev.at[:, far_cut], 1, 0)
    side_load.wait()
    edge_load.wait()
    for pair in loads:
        for load in pair:
            load.wait()
    for part in range(halves):
        start_rows(part, (0, pairs - 1))
    for i in range(height):
        start_ring(i)
    own_ring = send_ring(0, 0, height, DEEP)
    near_ring = send_ring(2, height - DEEP, DEEP, DEEP + height)
    far_ring = send_ring(1, 0, REACH + 1, 0)
    far_rows = []
    for part in range(halves):
        start_rows(part, range(1, pairs - 1))
        if part == 0:
            for begin, end in zip(CUTS[:2], CUTS[1:3]):
                far_rows.append([send_rows(first, 1, begin, end - begin, begin)])
    near_rows = [
        send_rows(ref, 2, height - DEEP, DEEP, DEEP + height) for ref in (first, ground)
    ]

    adj_load.wait()
    lane_tile = lax.broadcasted_iota(jnp.int32, (n_tiles, padded), 1)
    linked = jnp.zeros((n_tiles, padded), jnp.float32)
    links = adj[...]
    for k in range(links.shape[1]):
        linked = jnp.where(links[:, k : k + 1] == lane_tile, 1.0, linked)
    own = lax.broadcasted_iota(jnp.int32, (n_tiles, padded), 0) == lane_tile
    linked = jnp.where(own, 1.0, linked)
    one_hop = linked
    if n_tiles < padded:
        one_hop = jnp.concatenate(
            [one_hop, jnp.zeros((padded - n_tiles, padded), jnp.float32)], axis=0
        )
    count = jnp.where(own, 0.0, 1.0)
    reach = linked
    for step in range(ROUNDS):
        count = count + (1.0 - reach)
        if step < ROUNDS - 1:
            reach = jnp.dot(reach, one_hop, preferred_element_type=jnp.float32)
            reach = jnp.where(reach > 0.5, 1.0, 0.0)
    hops[...] = count

    def finish_ring(i, own_row, only=None):
        at = slot(i)
        for number, ref in enumerate((first, ground)):
            if only is not None and ref is not only:
                continue
            for p in (0, 1):
                ring = ring_own[2 * number + p, i] if own_row else ring_of(ref, at, p)
                from_high = jnp.broadcast_to(ring_high[2 * number + p, at], (SUBL, TILE))
                from_low = jnp.broadcast_to(ring_low[2 * number + p, at], (SUBL, TILE))
                ring = jnp.where(at_high, from_high, jnp.where(at_low, from_low, ring))
                put_tile(ref, at, tiles + p, ring)

    def state(k):
        return first if k == 0 else ping if k % 2 else pong

    all_tiles = range(tiles + 2)
    lowest_lane = lane_id == 0
    highest_lane = lane_id == TILE - 1

    def row_tiles(ref, at):
        return [tile_of(ref, at, v) for v in all_tiles]

    def lower(*rows):
        return [functools.reduce(jnp.minimum, tiles_at) for tiles_at in zip(*rows)]

    def least_of(low):
        even, odd = low[0::2], low[1::2]
        count = len(even)
        up = [pltpu.roll(each, 1, 1) for each in odd]
        down = [pltpu.roll(each, TILE - 1, 1) for each in even]
        least = []
        for g in range(count):
            both_of = jnp.minimum(even[g], odd[g])
            before = up[g] if count == 1 else jnp.where(lowest_lane, up[g - 1], up[g])
            after = down[g] if count == 1 else jnp.where(highest_lane, down[(g + 1) % count], down[g])
            least += [jnp.minimum(both_of, before), jnp.minimum(both_of, after)]
        return least

    def relax(k, begin, end):
        src, dst = state(k - 1), state(k)
        for at in range(begin, end, 2):
            count = min(2, end - at)
            rows = []
            for i in range(at - 1, at + count + 1):
                if i == -1 - REACH and k > 1:
                    rows.append(row_tiles(times_in, k - 2))
                else:
                    rows.append(row_tiles(src, slot(i)))
            for j in range(count):
                above, here, below = rows[j : j + 3]
                if count == 2:
                    middle = lower(rows[1], rows[2]) if j == 0 else middle
                    least = least_of(lower(middle, above if j == 0 else below))
                else:
                    least = least_of(lower(above, below, here))
                values = []
                for v in range(tiles if k == DEEP else tiles + 2):
                    rock = tile_of(ground, slot(at + j), v)
                    values.append(jnp.maximum(rock, jnp.minimum(here[v], least[v] + rise_step)))
                if k == DEEP:
                    finish_row(at + j, values)
                    continue
                for v, value in enumerate(values):
                    put_tile(dst, slot(at + j), v, value)
                if k == PASSES and 0 <= at + j < height:
                    column_floor[0] = jnp.minimum(column_floor[0], values[0])
                    column_floor[1] = jnp.minimum(column_floor[1], values[tiles - 1])

    def finish_row(i, values):
        if i >= FINAL:
            moved = shuffled([(values[2 * g], values[2 * g + 1]) for g in range(pairs)], join)
            values = [each for pair in moved for each in pair]
        for v, value in enumerate(values):
            put_tile(state(DEEP), slot(i), v, value)

    for entry in own_ring:
        arrive(entry)
    for i in range(height):
        finish_ring(i, True)
    far_times = []
    for k in range(1, height // 2):
        relax(k, k, height - k)
        if k < REACH:
            for v, value in enumerate(row_tiles(state(k), slot(REACH))):
                put_tile(times_out, k - 1, v, value)
            far_times.append(send(times_out.at[k - 1], times_in.at[k - 1], 1, 0))
    far_rows += [far_times[0:1], far_times[1:3], far_times[3:]]

    for entry in near_rows + near_ring:
        arrive(entry)
    for i in range(height, height + DEEP):
        finish_ring(i, False)
    for k in range(1, PASSES + 1):
        relax(k, height - k, height + PASSES - k)

    def strip(number, passes):
        for k in passes:
            relax(k, max(k - CUTS[number + 1], -REACH), k - CUTS[number])

    def open_strip(number):
        for entry in far_rows[number]:
            arrive(entry)
        if number == 1:
            for i in range(-CUTS[2], -CUTS[1]):
                finish_ring(i, False, first)

    for entry in far_ring + [far_ground]:
        arrive(entry)

    def far_start(flip):
        for g in range(pairs):
            rock = [turned([far_elev[number_of(0, s, 2 * g + p)] for s in range(SUBL)]) for p in (0, 1)]
            moved = shuffled(list(zip(*rock)), split)
            for r, pair in enumerate(moved):
                i = -1 - (r if flip else SUBL - 1 - r)
                for p in (0, 1):
                    if i >= -REACH:
                        put_tile(ground, slot(i), 2 * g + p, pair[p])

    by_side(far_start)
    for i in range(-REACH, 0):
        finish_ring(i, False, ground)

    for entry in far_rows[0]:
        arrive(entry)
    for i in range(-CUTS[1], 0):
        finish_ring(i, False, first)
    for k in range(1, PASSES + 1):
        strip(0, (k,))
        relax(k, height + PASSES - k, height + DEEP - k)
    for number in (1, 2):
        open_strip(number)
        strip(number, range(1, PASSES + 1))

    floor = jnp.minimum(
        jnp.where(first_cell, column_floor[0], unreached),
        jnp.where(last_cell, column_floor[1], unreached),
    )
    for v in range(tiles):
        floor = jnp.minimum(floor, tile_of(state(PASSES), slot(0), v))
    floor = jnp.min(floor, axis=(0, 1), keepdims=True)
    tile_id = tile_row * n_cols + col
    mine[...] = jnp.where(
        lax.broadcasted_iota(jnp.int32, (1, padded), 1) == tile_id,
        jnp.broadcast_to(floor, (1, padded)),
        unreached,
    )

    def level_copy(step):
        return pltpu.make_async_remote_copy(
            src_ref=mine,
            dst_ref=gathered.at[members - 1 - step],
            send_sem=level_send,
            recv_sem=level_recv,
            device_id=member((me + step) % members),
            device_id_type=MESH,
        )

    def spread(step, carry):
        level_copy(step).start()
        return carry

    lax.fori_loop(1, members, spread, 0)

    for k in range(PASSES + 1, DEEP + 1):
        relax(k, k - PASSES, height + DEEP - k)

    def walk_at(n, r):
        return n * (n - 1) // 2 + r

    outside_ring_cells = jnp.logical_or(at_high, at_low)
    entry_row = row_tiles(ground, slot(-1))
    for v in (tiles, tiles + 1):
        entry_row[v] = jnp.where(outside_ring_cells, unreached, entry_row[v])
    before = [entry_row]
    for n in range(1, FINAL + 1):
        after = []
        for r in range(n):
            least = least_of(lower(*before[max(r - 1, 0) : r + 2]))
            rock = row_tiles(ground, slot(r))
            after.append([jnp.maximum(rock[v], least[v] + rise_step) for v in all_tiles])
            for v in range(tiles):
                put_tile(walks, walk_at(n, r), v, after[r][v])
        before = after

    def seam_of(ref, at, p):
        ring = tile_of(ref, at, tiles + p)
        at_first = jnp.where(right_half, tile_of(ref, at, p), ring)
        at_last = jnp.where(right_half, ring, tile_of(ref, at, tiles - 2 + p))
        return jnp.where(sub_id == 0, at_first, at_last)

    seam_rows = list(range(-FINAL, height + FINAL))
    moved = shuffled([(seam_of(ground, slot(i), 0), seam_of(ground, slot(i), 1)) for i in seam_rows], join)
    for j, pair in enumerate(moved):
        seam_ground[j] = jnp.where(right_half, pair[0], pair[1])
    for number in (3, 4):
        open_strip(number)
        strip(number, range(1, DEEP + 1))

    pltpu.make_async_copy(gathered, gathered, level_recv).wait()
    row = jnp.minimum(mine[...], jnp.min(gathered[...], axis=0))
    count = hops[...]
    best = jnp.full((n_tiles, padded), unreached, jnp.float32)
    for step in range(ROUNDS + 1):
        best = jnp.minimum(
            best, jnp.where(count == float(step), jnp.broadcast_to(row, best.shape), unreached)
        )
        row = row + hop_rise
    level = jnp.min(best, axis=1, keepdims=True)
    levels[...] = jnp.broadcast_to(level + spill_lift, levels.shape)

    def ceiling(row_at, col_at):
        at = jnp.clip(row_at, 0, n_rows - 1) * n_cols + jnp.clip(col_at, 0, n_cols - 1)
        return jnp.broadcast_to(levels[pl.ds(at, 1)], (SUBL, TILE))

    def ceilings(row_at):
        here = ceiling(row_at, col)
        beside = jnp.where(
            at_high, ceiling(row_at, col + 1), jnp.where(at_low, ceiling(row_at, col - 1), here)
        )
        return here, beside

    own_top, own_beside = ceilings(tile_row)
    far_top, far_beside = ceilings(tile_row + far)

    seam = []
    for j, i in enumerate(seam_rows):
        seam.append(jnp.maximum(seam_ground[j], far_beside if i < 0 else own_beside))
    for k in range(1, FINAL + 1):
        later = list(seam)
        for j in range(k, len(seam) - k):
            low = jnp.minimum(jnp.minimum(seam[j - 1], seam[j + 1]), seam[j])
            least = jnp.minimum(low, jnp.minimum(pltpu.roll(low, 1, 1), pltpu.roll(low, TILE - 1, 1)))
            later[j] = jnp.maximum(seam_ground[j], jnp.minimum(seam[j], least + rise_step))
        seam = later

    for i in range(height):
        row = pl.ds(row_of(i), 1)
        seam_sides[0, row, :] = seam[i + FINAL][0:1]
        seam_sides[1, row, :] = seam[i + FINAL][SUBL - 1 : SUBL]
    tops = []
    for n in range(1, FINAL + 1):
        far_top = far_top + rise_step
        tops.append(far_top)
    blocks = []
    for i in range(FINAL):
        values = row_tiles(state(DEEP), slot(i))
        for v in range(tiles):
            for n in range(i + 1, FINAL + 1):
                walk = tile_of(walks, walk_at(n, i), v)
                values[v] = jnp.minimum(values[v], jnp.maximum(walk, tops[n - 1]))
        blocks += [(values[2 * g], values[2 * g + 1]) for g in range(pairs)]
    moved = shuffled(blocks, join)
    for i in range(FINAL):
        for v in range(tiles):
            put_tile(state(DEEP), slot(i), v, moved[i * pairs + v // 2][v % 2])

    def finish(flip):
        for half in (range(halves - 1, -1, -1) if not flip else range(halves)):
            for v in range(tiles):
                order = [half * SUBL + r for r in range(SUBL)]
                order = [height - 1 - row if flip else row for row in order]
                rows = turned([tile_of(state(DEEP), slot(i), v) for i in order])
                for s in range(SUBL):
                    at = number_of(half, s, v)
                    value = jnp.minimum(rows[s], jnp.maximum(elev[at], own_top))
                    at_half = slice(half * SUBL, (half + 1) * SUBL)
                    if s == 0 and v == 0:
                        left = jnp.minimum(value, seam_sides[0, at_half, :])
                        value = jnp.where(lane_id < FINAL, left, value)
                    if s == SUBL - 1 and v == tiles - 1:
                        right = jnp.minimum(value, seam_sides[1, at_half, :])
                        value = jnp.where(lane_id >= TILE - FINAL, right, value)
                    out[at] = value

    by_side(finish)

    for copy, side_of, dc in copies:
        when(both(side_of, dc), copy.wait_send)
    pltpu.make_async_copy(gathered, gathered, level_send).wait()


def per_device(sizes, elevation, fill_depth, edge_rows, edge_sides, adjacency):
    height, width = elevation.shape
    chunk = width // SUBL
    tiles = width // TILE
    total = height + 2 * DEEP
    members = sizes[1] * sizes[2] * sizes[3]
    n_tiles = adjacency.shape[0]
    padded = -(-n_tiles // TILE) * TILE
    flat = (height * tiles // SUBL, SUBL, TILE)

    def tiled(array):
        blocks = array.reshape(height // SUBL, SUBL, tiles, TILE)
        return blocks.transpose(0, 2, 1, 3).reshape(flat)

    wide = pltpu.VMEM((total, SUBL, chunk + 2 * TILE), jnp.float32)
    shuffle = pltpu.VMEM((2 * TILE, 2 * TILE), jnp.bfloat16)
    whole = pltpu.VMEM(flat, jnp.float32)
    times = pltpu.VMEM((REACH - 1, SUBL, chunk + 2 * TILE), jnp.float32)
    ring = pltpu.VMEM((4, total, 1, TILE), jnp.float32)
    marks = edge_rows.reshape(2, tiles, TILE).transpose(1, 0, 2).reshape(2 * tiles, TILE)
    operands = (tiled(elevation), tiled(fill_depth), marks, edge_sides, adjacency)
    filled = pl.pallas_call(
        functools.partial(kernel, sizes),
        out_shape=pltpu.VMEM(flat, jnp.float32),
        in_specs=[pl.BlockSpec(memory_space=pltpu.HBM)] * 5,
        out_specs=pl.BlockSpec(memory_space=pltpu.VMEM),
        scratch_shapes=[
            whole, whole,
            pltpu.VMEM((tiles, SUBL, TILE), jnp.float32),
            wide, wide, wide, wide,
            pltpu.VMEM((FINAL * (FINAL + 1) // 2, SUBL, chunk), jnp.float32),
            times, times,
            pltpu.VMEM((2 * tiles, TILE), jnp.int32),
            pltpu.SMEM(edge_sides.shape, jnp.int32),
            pltpu.VMEM(adjacency.shape, jnp.int32),
            pltpu.VMEM((4, height, SUBL, TILE), jnp.float32),
            ring, ring,
            pltpu.VMEM((2, SUBL, TILE), jnp.float32),
            pltpu.VMEM((1, padded), jnp.float32),
            pltpu.VMEM((members - 1, 1, padded), jnp.float32),
            pltpu.VMEM((n_tiles, padded), jnp.float32),
            pltpu.VMEM((n_tiles, TILE), jnp.float32),
            pltpu.VMEM((height + 2 * FINAL, SUBL, TILE), jnp.float32),
            pltpu.VMEM((2, height, TILE), jnp.float32),
            shuffle, shuffle,
            pltpu.SemaphoreType.DMA((2 * (height // SUBL) + 3,)),
            pltpu.SemaphoreType.DMA((16,)),
            pltpu.SemaphoreType.DMA((16,)),
            pltpu.SemaphoreType.DMA,
            pltpu.SemaphoreType.DMA,
        ],
        compiler_params=pltpu.CompilerParams(
            collective_id=0, has_side_effects=True, vmem_limit_bytes=32 * 1024 * 1024
        ),
    )(*(pltpu.with_memory_space_constraint(each, pltpu.HBM) for each in operands))
    blocks = filled.reshape(height // SUBL, tiles, SUBL, TILE)
    return blocks.transpose(0, 2, 1, 3).reshape(height, width)


def solution(mesh):
    sizes = tuple(mesh.shape[name] for name in ("groups", "rows", "cols", "sub"))
    placed = (
        P(("groups", "rows", "sub"), "cols"),
        P(("groups", "rows", "sub"), "cols"),
        P("groups", "cols"),
        P("groups", ("rows", "sub")),
        P("groups", None),
    )
    return jax.shard_map(
        functools.partial(per_device, sizes),
        mesh=mesh,
        in_specs=placed,
        out_specs=P(("groups", "rows", "sub"), "cols"),
        check_vma=False,
    )
```

```python
import functools

import jax
import jax.numpy as jnp
from jax import lax
from jax.experimental import pallas as pl
from jax.experimental.pallas import tpu as pltpu
from jax.sharding import PartitionSpec as P

PASSES = 8
FINAL = 4
ROUNDS = 4

unreached = 1000000000.0
rise_step = 0.01
hop_rise = 0.05
spill_lift = 3.0

DEEP = PASSES + FINAL
REACH = DEEP // 2
CUTS = (0, 4, REACH + 1, PASSES, PASSES + 2, DEEP)
MOST_UNROLLED = 16
SUBL = 8
TILE = 128
HALF = TILE // 2
MESH = pl.DeviceIdType.MESH


def kernel(
    sizes, elev_hbm, fill_hbm, edge_hbm, side_hbm, adj_hbm, out,
    elev, fill, far_elev, ground, first, ping, pong, walks, times_out, times_in,
    edge, side, adj, ring_own, ring_low, ring_high, column_floor,
    mine, gathered, hops, levels, seam_ground, seam_sides, split, join,
    load_sem, send_sem, recv_sem, level_send, level_recv,
):
    n_groups, n_rows, n_cols, n_sub = sizes
    tiles = edge_hbm.shape[0] // (2 * SUBL)
    chunk = tiles * TILE
    pairs = tiles // 2
    lanes = chunk + 2 * TILE
    half_tiles = tiles * SUBL
    half_rows = SUBL * half_tiles
    halves = elev_hbm.shape[0] // half_tiles
    height = halves * SUBL
    n_tiles = adj.shape[0]
    padded = mine.shape[1]
    members = n_rows * n_cols * n_sub

    group = lax.axis_index("groups")
    tile_row = lax.axis_index("rows")
    col = lax.axis_index("cols")
    sub = lax.axis_index("sub")
    band = tile_row * n_sub + sub
    bands = n_rows * n_sub
    me = (tile_row * n_cols + col) * n_sub + sub

    near = 1 - 2 * sub
    far = -near

    def row_of(i):
        return jnp.where(sub == 0, i, height - 1 - i)

    def slot(i):
        if i < 0:
            return -1 - i
        if i < height:
            return DEEP + i
        return 2 * DEEP + 2 * height - 1 - i

    def has(dr):
        return jnp.logical_and(band + dr >= 0, band + dr < bands)

    has_col = {-1: col > 0, 1: col < n_cols - 1}

    def both(side_of, dc):
        there = {0: None, 1: has(far), 2: None}[side_of]
        if dc == 0:
            return there
        return has_col[dc] if there is None else jnp.logical_and(there, has_col[dc])

    def device(side_of, dc):
        to_band = band + {0: 0, 1: far, 2: near}[side_of]
        return (group, to_band // n_sub, col + dc, to_band % n_sub)

    def when(condition, action):
        if condition is None:
            action()
        else:
            pl.when(condition)(action)

    barrier = pltpu.get_barrier_semaphore()

    def member(number):
        return (group, number // (n_sub * n_cols), (number // n_sub) % n_cols, number % n_sub)

    def greet(step, carry):
        apart = step
        pl.semaphore_signal(
            barrier, inc=1, device_id=member((me + apart) % members), device_id_type=MESH
        )
        return carry

    lax.fori_loop(1, members, greet, 0, unroll=members <= MOST_UNROLLED)
    loads = []
    for part in range(halves):
        half = row_of(part * SUBL) // SUBL
        at = pl.ds(half * half_tiles, half_tiles)
        pair = []
        for number, (src, dst) in enumerate(((elev_hbm, elev), (fill_hbm, fill))):
            copy = pltpu.make_async_copy(src.at[at], dst.at[at], load_sem.at[2 * part + number])
            copy.start()
            pair.append(copy)
        loads.append(pair)
    spare = 2 * halves
    side_load = pltpu.make_async_copy(side_hbm, side, load_sem.at[spare])
    side_load.start()
    edge_load = pltpu.make_async_copy(edge_hbm, edge, load_sem.at[spare + 1])
    edge_load.start()
    adj_load = pltpu.make_async_copy(adj_hbm, adj, load_sem.at[spare + 2])
    adj_load.start()

    def outside_rows():
        for ref in (ground, first):
            ref[0:DEEP] = jnp.full((DEEP, SUBL, lanes), unreached, jnp.float32)
        for ref in (far_elev, times_in):
            ref[...] = jnp.full(ref.shape, unreached, jnp.float32)

    pl.when(jnp.logical_not(has(far)))(outside_rows)

    spans = {0: (DEEP, height), 1: (0, DEEP), 2: (DEEP + height, DEEP)}
    for dc, ref in ((-1, ring_low), (1, ring_high)):
        for side_of in (0, 1, 2):

            def outside_ring(ref=ref, side_of=side_of):
                at, count = spans[side_of]
                ref[:, at : at + count] = jnp.full((4, count, 1, TILE), unreached, jnp.float32)

            pl.when(jnp.logical_not(both(side_of, dc)))(outside_ring)
    column_floor[...] = jnp.full(column_floor.shape, unreached, jnp.float32)

    sub_id = lax.broadcasted_iota(jnp.int32, (SUBL, TILE), 0)
    lane_id = lax.broadcasted_iota(jnp.int32, (SUBL, TILE), 1)
    first_cell = jnp.logical_and(sub_id == 0, lane_id == 0)
    last_cell = jnp.logical_and(sub_id == SUBL - 1, lane_id == TILE - 1)
    is_first_col = (col == 0).astype(jnp.int32)
    is_last_col = (col == n_cols - 1).astype(jnp.int32)
    at_slab_edge = jnp.where(has(far), 2, 1)
    right_half = lane_id < HALF
    at_high = jnp.logical_and(sub_id == SUBL - 1, right_half)
    at_low = jnp.logical_and(sub_id == 0, jnp.logical_not(right_half))

    near_id = lax.broadcasted_iota(jnp.int32, (2 * TILE, 2 * TILE), 0)
    pair_id = lax.broadcasted_iota(jnp.int32, (2 * TILE, 2 * TILE), 1)
    split[...] = (near_id == 2 * (pair_id % TILE) + pair_id // TILE).astype(jnp.bfloat16)
    join[...] = (pair_id == 2 * (near_id % TILE) + near_id // TILE).astype(jnp.bfloat16)

    def shuffled(blocks, order):
        whole = jnp.concatenate([jnp.concatenate(block, axis=1) for block in blocks], axis=0)
        total = None
        for term in range(3):
            part = whole.astype(jnp.bfloat16)
            whole = whole - part.astype(jnp.float32)
            moved = jnp.dot(part, order[...], preferred_element_type=jnp.float32)
            total = moved if total is None else total + moved
        return [
            (total[SUBL * b : SUBL * (b + 1), 0:TILE], total[SUBL * b : SUBL * (b + 1), TILE : 2 * TILE])
            for b in range(len(blocks))
        ]

    def tile_of(ref, at, v):
        return ref[at, :, v * TILE : (v + 1) * TILE]

    def put_tile(ref, at, v, value):
        ref[at, :, v * TILE : (v + 1) * TILE] = value

    def ring_of(ref, at, p):
        return jnp.where(
            right_half,
            pltpu.roll(tile_of(ref, at, p), SUBL - 1, 0),
            pltpu.roll(tile_of(ref, at, tiles - 2 + p), 1, 0),
        )

    def turned(rows):
        rows = list(rows)
        for step in (4, 2, 1):
            stays = sub_id % (2 * step) < step
            for at in range(SUBL):
                if at % (2 * step) < step:
                    one, two = rows[at], rows[at + step]
                    rows[at] = jnp.where(stays, one, pltpu.roll(two, step, 0))
                    rows[at + step] = jnp.where(stays, pltpu.roll(one, SUBL - step, 0), two)
        return rows

    def number_of(half, s, v):
        return half * half_tiles + s * tiles + v

    def by_side(action):
        pl.when(sub == 0)(lambda: action(False))
        pl.when(sub == 1)(lambda: action(True))

    def start_rows(part, groups):
        def action(flip):
            half = halves - 1 - part if flip else part
            for g in groups:
                here, water = {}, {}
                for v in (2 * g, 2 * g + 1):
                    rock = [elev[number_of(half, s, v)] for s in range(SUBL)]
                    deep = [rock[s] + fill[number_of(half, s, v)] for s in range(SUBL)]
                    here[v], water[v] = turned(rock), turned(deep)
                    for r in range(SUBL):
                        row = half * SUBL + r
                        if row == (height - 1 if flip else 0):
                            marks = edge[pl.ds(2 * v + flip, SUBL, stride=2 * tiles), :]
                            water[v][r] = jnp.where(marks == at_slab_edge, here[v][r], water[v][r])
                        if v == 0:
                            mark = jnp.where(first_cell, side[0, row] * is_first_col, 0) == 1
                            water[v][r] = jnp.where(mark, here[v][r], water[v][r])
                        if v == tiles - 1:
                            mark = jnp.where(last_cell, side[1, row] * is_last_col, 0) == 1
                            water[v][r] = jnp.where(mark, here[v][r], water[v][r])
                for ref, array in ((ground, here), (first, water)):
                    moved = shuffled([(array[2 * g][r], array[2 * g + 1][r]) for r in range(SUBL)], split)
                    for r, pair in enumerate(moved):
                        row = half * SUBL + r
                        for p in (0, 1):
                            put_tile(ref, slot(height - 1 - row if flip else row), 2 * g + p, pair[p])

        by_side(action)

    def start_ring(i):
        for number, ref in enumerate((first, ground)):
            for p in (0, 1):
                ring_own[2 * number + p, i] = ring_of(ref, slot(i), p)

    copies = []

    def send(src, dst, side_of, dc):
        number = len(copies)
        copy = pltpu.make_async_remote_copy(
            src_ref=src,
            dst_ref=dst,
            send_sem=send_sem.at[number],
            recv_sem=recv_sem.at[number],
            device_id=device(side_of, dc),
            device_id_type=MESH,
        )
        when(both(side_of, dc), copy.start)
        copies.append((copy, side_of, dc))
        return copy, side_of, dc

    def arrive(entry):
        copy, side_of, dc = entry
        when(both(side_of, -dc), copy.wait_recv)

    def send_rows(ref, side_of, i, count, to):
        return send(
            ref.at[pl.ds(slot(i), count), :, pl.ds(0, chunk)],
            ref.at[pl.ds(to, count), :, pl.ds(0, chunk)],
            side_of, 0,
        )

    def send_ring(side_of, i, count, to):
        sent = []
        for dc in (-1, 1):
            target = ring_high if dc == -1 else ring_low
            part = SUBL - 1 if dc == -1 else 0
            sent.append(
                send(
                    ring_own.at[:, pl.ds(i, count), pl.ds(part, 1)],
                    target.at[:, pl.ds(to, count)],
                    side_of, dc,
                )
            )
        return sent

    pl.semaphore_wait(barrier, members - 1)
    far_half = pl.ds((row_of(0) // SUBL) * half_tiles, half_tiles)
    far_cut = pl.ds(jnp.where(sub == 0, 0, SUBL - REACH), REACH)
    far_ground = send(elev_hbm.at[far_half, far_cut], far_elev.at[:, far_cut], 1, 0)
    side_load.wait()
    edge_load.wait()
    for pair in loads:
        for load in pair:
            load.wait()
    for part in range(halves):
        start_rows(part, (0, pairs - 1))
    for i in range(height):
        start_ring(i)
    own_ring = send_ring(0, 0, height, DEEP)
    near_ring = send_ring(2, height - DEEP, DEEP, DEEP + height)
    far_ring = send_ring(1, 0, REACH + 1, 0)
    far_rows = []
    for part in range(halves):
        start_rows(part, range(1, pairs - 1))
        if part == 0:
            for begin, end in zip(CUTS[:2], CUTS[1:3]):
                far_rows.append([send_rows(first, 1, begin, end - begin, begin)])
    near_rows = [
        send_rows(ref, 2, height - DEEP, DEEP, DEEP + height) for ref in (first, ground)
    ]

    adj_load.wait()
    lane_tile = lax.broadcasted_iota(jnp.int32, (n_tiles, padded), 1)
    linked = jnp.zeros((n_tiles, padded), jnp.float32)
    links = adj[...]
    for k in range(links.shape[1]):
        linked = jnp.where(links[:, k : k + 1] == lane_tile, 1.0, linked)
    own = lax.broadcasted_iota(jnp.int32, (n_tiles, padded), 0) == lane_tile
    linked = jnp.where(own, 1.0, linked)
    one_hop = linked
    if n_tiles < padded:
        one_hop = jnp.concatenate(
            [one_hop, jnp.zeros((padded - n_tiles, padded), jnp.float32)], axis=0
        )
    count = jnp.where(own, 0.0, 1.0)
    reach = linked
    for step in range(ROUNDS):
        count = count + (1.0 - reach)
        if step < ROUNDS - 1:
            reach = jnp.dot(reach, one_hop, preferred_element_type=jnp.float32)
            reach = jnp.where(reach > 0.5, 1.0, 0.0)
    hops[...] = count

    def finish_ring(i, own_row, only=None):
        at = slot(i)
        for number, ref in enumerate((first, ground)):
            if only is not None and ref is not only:
                continue
            for p in (0, 1):
                ring = ring_own[2 * number + p, i] if own_row else ring_of(ref, at, p)
                from_high = jnp.broadcast_to(ring_high[2 * number + p, at], (SUBL, TILE))
                from_low = jnp.broadcast_to(ring_low[2 * number + p, at], (SUBL, TILE))
                ring = jnp.where(at_high, from_high, jnp.where(at_low, from_low, ring))
                put_tile(ref, at, tiles + p, ring)

    def state(k):
        return first if k == 0 else ping if k % 2 else pong

    all_tiles = range(tiles + 2)
    lowest_lane = lane_id == 0
    highest_lane = lane_id == TILE - 1

    def row_tiles(ref, at):
        return [tile_of(ref, at, v) for v in all_tiles]

    def lower(*rows):
        return [functools.reduce(jnp.minimum, tiles_at) for tiles_at in zip(*rows)]

    def least_of(low):
        even, odd = low[0::2], low[1::2]
        count = len(even)
        up = [pltpu.roll(each, 1, 1) for each in odd]
        down = [pltpu.roll(each, TILE - 1, 1) for each in even]
        least = []
        for g in range(count):
            both_of = jnp.minimum(even[g], odd[g])
            before = up[g] if count == 1 else jnp.where(lowest_lane, up[g - 1], up[g])
            after = down[g] if count == 1 else jnp.where(highest_lane, down[(g + 1) % count], down[g])
            least += [jnp.minimum(both_of, before), jnp.minimum(both_of, after)]
        return least

    def relax(k, begin, end):
        src, dst = state(k - 1), state(k)
        for at in range(begin, end, 2):
            count = min(2, end - at)
            rows = []
            for i in range(at - 1, at + count + 1):
                if i == -1 - REACH and k > 1:
                    rows.append(row_tiles(times_in, k - 2))
                else:
                    rows.append(row_tiles(src, slot(i)))
            for j in range(count):
                above, here, below = rows[j : j + 3]
                if count == 2:
                    middle = lower(rows[1], rows[2]) if j == 0 else middle
                    least = least_of(lower(middle, above if j == 0 else below))
                else:
                    least = least_of(lower(above, below, here))
                values = []
                for v in range(tiles if k == DEEP else tiles + 2):
                    rock = tile_of(ground, slot(at + j), v)
                    values.append(jnp.maximum(rock, jnp.minimum(here[v], least[v] + rise_step)))
                if k == DEEP:
                    finish_row(at + j, values)
                    continue
                for v, value in enumerate(values):
                    put_tile(dst, slot(at + j), v, value)
                if k == PASSES and 0 <= at + j < height:
                    column_floor[0] = jnp.minimum(column_floor[0], values[0])
                    column_floor[1] = jnp.minimum(column_floor[1], values[tiles - 1])

    def finish_row(i, values):
        if i >= FINAL:
            moved = shuffled([(values[2 * g], values[2 * g + 1]) for g in range(pairs)], join)
            values = [each for pair in moved for each in pair]
        for v, value in enumerate(values):
            put_tile(state(DEEP), slot(i), v, value)

    for entry in own_ring:
        arrive(entry)
    for i in range(height):
        finish_ring(i, True)
    far_times = []
    for k in range(1, height // 2):
        relax(k, k, height - k)
        if k < REACH:
            for v, value in enumerate(row_tiles(state(k), slot(REACH))):
                put_tile(times_out, k - 1, v, value)
            far_times.append(send(times_out.at[k - 1], times_in.at[k - 1], 1, 0))
    far_rows += [far_times[0:1], far_times[1:3], far_times[3:]]

    for entry in near_rows + near_ring:
        arrive(entry)
    for i in range(height, height + DEEP):
        finish_ring(i, False)
    for k in range(1, PASSES + 1):
        relax(k, height - k, height + PASSES - k)

    def strip(number, passes):
        for k in passes:
            relax(k, max(k - CUTS[number + 1], -REACH), k - CUTS[number])

    def open_strip(number):
        for entry in far_rows[number]:
            arrive(entry)
        if number == 1:
            for i in range(-CUTS[2], -CUTS[1]):
                finish_ring(i, False, first)

    for entry in far_ring + [far_ground]:
        arrive(entry)

    def far_start(flip):
        for g in range(pairs):
            rock = [turned([far_elev[number_of(0, s, 2 * g + p)] for s in range(SUBL)]) for p in (0, 1)]
            moved = shuffled(list(zip(*rock)), split)
            for r, pair in enumerate(moved):
                i = -1 - (r if flip else SUBL - 1 - r)
                for p in (0, 1):
                    if i >= -REACH:
                        put_tile(ground, slot(i), 2 * g + p, pair[p])

    by_side(far_start)
    for i in range(-REACH, 0):
        finish_ring(i, False, ground)

    for entry in far_rows[0]:
        arrive(entry)
    for i in range(-CUTS[1], 0):
        finish_ring(i, False, first)
    for k in range(1, PASSES + 1):
        strip(0, (k,))
        relax(k, height + PASSES - k, height + DEEP - k)
    def seam_of(ref, at, p):
        ring = tile_of(ref, at, tiles + p)
        at_first = jnp.where(right_half, tile_of(ref, at, p), ring)
        at_last = jnp.where(right_half, ring, tile_of(ref, at, tiles - 2 + p))
        return jnp.where(sub_id == 0, at_first, at_last)

    seam_rows = list(range(-FINAL, height + FINAL))
    moved = shuffled([(seam_of(ground, slot(i), 0), seam_of(ground, slot(i), 1)) for i in seam_rows], join)
    for j, pair in enumerate(moved):
        seam_ground[j] = jnp.where(right_half, pair[0], pair[1])
    for number in (1, 2):
        open_strip(number)
        strip(number, range(1, PASSES + 1))

    floor = jnp.minimum(
        jnp.where(first_cell, column_floor[0], unreached),
        jnp.where(last_cell, column_floor[1], unreached),
    )
    for v in range(tiles):
        floor = jnp.minimum(floor, tile_of(state(PASSES), slot(0), v))
    floor = jnp.min(floor, axis=(0, 1), keepdims=True)
    tile_id = tile_row * n_cols + col
    mine[...] = jnp.where(
        lax.broadcasted_iota(jnp.int32, (1, padded), 1) == tile_id,
        jnp.broadcast_to(floor, (1, padded)),
        unreached,
    )

    def level_copy(step):
        return pltpu.make_async_remote_copy(
            src_ref=mine,
            dst_ref=gathered.at[members - 1 - step],
            send_sem=level_send,
            recv_sem=level_recv,
            device_id=member((me + step) % members),
            device_id_type=MESH,
        )

    def spread(step, carry):
        level_copy(step).start()
        return carry

    lax.fori_loop(1, members, spread, 0, unroll=members <= MOST_UNROLLED)

    for k in range(PASSES + 1, DEEP + 1):
        relax(k, k - PASSES, height + DEEP - k)

    def walk_at(n, r):
        return n * (n - 1) // 2 + r

    outside_ring_cells = jnp.logical_or(at_high, at_low)
    entry_row = row_tiles(ground, slot(-1))
    for v in (tiles, tiles + 1):
        entry_row[v] = jnp.where(outside_ring_cells, unreached, entry_row[v])
    before = [entry_row]
    for n in range(1, FINAL + 1):
        after = []
        for r in range(n):
            least = least_of(lower(*before[max(r - 1, 0) : r + 2]))
            rock = row_tiles(ground, slot(r))
            after.append([jnp.maximum(rock[v], least[v] + rise_step) for v in all_tiles])
            for v in range(tiles):
                put_tile(walks, walk_at(n, r), v, after[r][v])
        before = after

    for number in (3, 4):
        open_strip(number)
        strip(number, range(1, DEEP + 1))

    pltpu.make_async_copy(gathered, gathered, level_recv).wait()
    row = jnp.minimum(mine[...], jnp.min(gathered[...], axis=0))
    count = hops[...]
    best = jnp.full((n_tiles, padded), unreached, jnp.float32)
    for step in range(ROUNDS + 1):
        best = jnp.minimum(
            best, jnp.where(count == float(step), jnp.broadcast_to(row, best.shape), unreached)
        )
        row = row + hop_rise
    level = jnp.min(best, axis=1, keepdims=True)
    levels[...] = jnp.broadcast_to(level + spill_lift, levels.shape)

    def ceiling(row_at, col_at):
        at = jnp.clip(row_at, 0, n_rows - 1) * n_cols + jnp.clip(col_at, 0, n_cols - 1)
        return jnp.broadcast_to(levels[pl.ds(at, 1)], (SUBL, TILE))

    def ceilings(row_at):
        here = ceiling(row_at, col)
        beside = jnp.where(
            at_high, ceiling(row_at, col + 1), jnp.where(at_low, ceiling(row_at, col - 1), here)
        )
        return here, beside

    own_top, own_beside = ceilings(tile_row)
    far_top, far_beside = ceilings(tile_row + far)

    seam = []
    for j, i in enumerate(seam_rows):
        seam.append(jnp.maximum(seam_ground[j], far_beside if i < 0 else own_beside))
    for k in range(1, FINAL + 1):
        later = list(seam)
        for j in range(k, len(seam) - k):
            low = jnp.minimum(jnp.minimum(seam[j - 1], seam[j + 1]), seam[j])
            least = jnp.minimum(low, jnp.minimum(pltpu.roll(low, 1, 1), pltpu.roll(low, TILE - 1, 1)))
            later[j] = jnp.maximum(seam_ground[j], jnp.minimum(seam[j], least + rise_step))
        seam = later

    for i in range(height):
        row = pl.ds(row_of(i), 1)
        seam_sides[0, row, :] = seam[i + FINAL][0:1]
        seam_sides[1, row, :] = seam[i + FINAL][SUBL - 1 : SUBL]
    tops = []
    for n in range(1, FINAL + 1):
        far_top = far_top + rise_step
        tops.append(far_top)
    blocks = []
    for i in range(FINAL):
        values = row_tiles(state(DEEP), slot(i))
        for v in range(tiles):
            for n in range(i + 1, FINAL + 1):
                walk = tile_of(walks, walk_at(n, i), v)
                values[v] = jnp.minimum(values[v], jnp.maximum(walk, tops[n - 1]))
        blocks += [(values[2 * g], values[2 * g + 1]) for g in range(pairs)]
    moved = shuffled(blocks, join)
    for i in range(FINAL):
        for v in range(tiles):
            put_tile(state(DEEP), slot(i), v, moved[i * pairs + v // 2][v % 2])

    def finish(flip):
        for half in (range(halves - 1, -1, -1) if not flip else range(halves)):
            for v in range(tiles):
                order = [half * SUBL + r for r in range(SUBL)]
                order = [height - 1 - row if flip else row for row in order]
                rows = turned([tile_of(state(DEEP), slot(i), v) for i in order])
                for s in range(SUBL):
                    at = number_of(half, s, v)
                    value = jnp.minimum(rows[s], jnp.maximum(elev[at], own_top))
                    at_half = slice(half * SUBL, (half + 1) * SUBL)
                    if s == 0 and v == 0:
                        left = jnp.minimum(value, seam_sides[0, at_half, :])
                        value = jnp.where(lane_id < FINAL, left, value)
                    if s == SUBL - 1 and v == tiles - 1:
                        right = jnp.minimum(value, seam_sides[1, at_half, :])
                        value = jnp.where(lane_id >= TILE - FINAL, right, value)
                    out[at] = value

    by_side(finish)

    for copy, side_of, dc in copies:
        when(both(side_of, dc), copy.wait_send)
    pltpu.make_async_copy(gathered, gathered, level_send).wait()


def per_device(sizes, elevation, fill_depth, edge_rows, edge_sides, adjacency):
    height, width = elevation.shape
    chunk = width // SUBL
    tiles = width // TILE
    total = height + 2 * DEEP
    members = sizes[1] * sizes[2] * sizes[3]
    n_tiles = adjacency.shape[0]
    padded = -(-n_tiles // TILE) * TILE
    flat = (height * tiles // SUBL, SUBL, TILE)

    def tiled(array):
        blocks = array.reshape(height // SUBL, SUBL, tiles, TILE)
        return blocks.transpose(0, 2, 1, 3).reshape(flat)

    wide = pltpu.VMEM((total, SUBL, chunk + 2 * TILE), jnp.float32)
    shuffle = pltpu.VMEM((2 * TILE, 2 * TILE), jnp.bfloat16)
    whole = pltpu.VMEM(flat, jnp.float32)
    times = pltpu.VMEM((REACH - 1, SUBL, chunk + 2 * TILE), jnp.float32)
    ring = pltpu.VMEM((4, total, 1, TILE), jnp.float32)
    marks = edge_rows.reshape(2, tiles, TILE).transpose(1, 0, 2).reshape(2 * tiles, TILE)
    operands = (tiled(elevation), tiled(fill_depth), marks, edge_sides, adjacency)
    filled = pl.pallas_call(
        functools.partial(kernel, sizes),
        out_shape=pltpu.VMEM(flat, jnp.float32),
        in_specs=[pl.BlockSpec(memory_space=pltpu.HBM)] * 5,
        out_specs=pl.BlockSpec(memory_space=pltpu.VMEM),
        scratch_shapes=[
            whole, whole,
            pltpu.VMEM((tiles, SUBL, TILE), jnp.float32),
            wide, wide, wide, wide,
            pltpu.VMEM((FINAL * (FINAL + 1) // 2, SUBL, chunk), jnp.float32),
            times, times,
            pltpu.VMEM((2 * tiles, TILE), jnp.int32),
            pltpu.SMEM(edge_sides.shape, jnp.int32),
            pltpu.VMEM(adjacency.shape, jnp.int32),
            pltpu.VMEM((4, height, SUBL, TILE), jnp.float32),
            ring, ring,
            pltpu.VMEM((2, SUBL, TILE), jnp.float32),
            pltpu.VMEM((1, padded), jnp.float32),
            pltpu.VMEM((members - 1, 1, padded), jnp.float32),
            pltpu.VMEM((n_tiles, padded), jnp.float32),
            pltpu.VMEM((n_tiles, TILE), jnp.float32),
            pltpu.VMEM((height + 2 * FINAL, SUBL, TILE), jnp.float32),
            pltpu.VMEM((2, height, TILE), jnp.float32),
            shuffle, shuffle,
            pltpu.SemaphoreType.DMA((2 * (height // SUBL) + 3,)),
            pltpu.SemaphoreType.DMA((16,)),
            pltpu.SemaphoreType.DMA((16,)),
            pltpu.SemaphoreType.DMA,
            pltpu.SemaphoreType.DMA,
        ],
        compiler_params=pltpu.CompilerParams(
            collective_id=0, has_side_effects=True, vmem_limit_bytes=32 * 1024 * 1024
        ),
    )(*(pltpu.with_memory_space_constraint(each, pltpu.HBM) for each in operands))
    blocks = filled.reshape(height // SUBL, tiles, SUBL, TILE)
    return blocks.transpose(0, 2, 1, 3).reshape(height, width)


def solution(mesh):
    sizes = tuple(mesh.shape[name] for name in ("groups", "rows", "cols", "sub"))
    placed = (
        P(("groups", "rows", "sub"), "cols"),
        P(("groups", "rows", "sub"), "cols"),
        P("groups", "cols"),
        P("groups", ("rows", "sub")),
        P("groups", None),
    )
    return jax.shard_map(
        functools.partial(per_device, sizes),
        mesh=mesh,
        in_specs=placed,
        out_specs=P(("groups", "rows", "sub"), "cols"),
        check_vma=False,
    )
```
